128 devices in a mesh: slab: 16 (over x, z), tile: 8 (over y, core).
Axes of the slice: x: 4, y: 4, z: 4, core: 2. Of those that a mesh axis runs over, the one named last changes fastest.
Arguments:
- encoded: bfloat16 [16, 16, 4096, 128], P('slab', None, 'tile'), may hold values from -6 to 6
- spacing: float32 [16, 16, 4096], P('slab', None, 'tile'), may hold values from 0.002 to 0.05
- counts: int32 [16, 4096], P('slab', 'tile'), may hold values from 1 to 16
- seg_first: int32 [4096], P('tile'), may hold values from 0 to 3
- seg_last: int32 [4096], P('tile'), may hold values from 13 to 16
- direction: int32 [4096], P('tile'), may hold values from 0 to 1
- field_in: bfloat16 [16, 128, 256], P('slab'), may hold values from -0.5 to 0.5
- field_mid: bfloat16 [16, 256, 256], P('slab'), may hold values from -0.375 to 0.375
- field_out: bfloat16 [16, 256, 64], P('slab'), may hold values from -0.375 to 0.375
- color_head: float32 [64, 3], replicated, may hold values from -0.75 to 0.75
- target: float32 [4096, 3], P('tile'), may hold values from 0 to 1
Outputs:
- front_trans: float32 [16, 4096], P('slab', 'tile')
- grad_in: float32 [16, 128, 256], P('slab')
- grad_mid: float32 [16, 256, 256], P('slab')
- grad_out: float32 [16, 256, 64], P('slab')
The draws below stay inside these ranges and needn't reach their ends.
All inputs are finite; a program needn't handle non-finite values.
Results may differ from the reference program's by a relative error of at most 0.014.
The reference program's roundings to bfloat16 on the way (of `hidden_one`, `hidden_two`, `grad_low`, `back_two` and `back_one`) count: a program that leaves them out, or rounds other values in their place, can miss the bound.
Values sent between devices are 32-bit elements; how exact they have to be, the bound alone decides.
A program may use at most 64 MiB of HBM per device.

```python
import math
import jax
import jax.numpy as jnp
from jax import lax

ENC = 128
HID = 256
OUT = 64
SAMP = 16
RAYS_DEV = 512
SLABS = 16
RAYS = 4096
N_SLAB = 16


def set_ends(values, stream_key, smallest, top_value):
    longest = values.shape.index(max(values.shape))
    spots = []
    for shift in (0, 1):
        where = [jax.random.randint(jax.random.fold_in(stream_key, axis), (), 0, length) for axis, length in enumerate(values.shape)]
        where[longest] = (where[longest] + shift) % values.shape[longest]
        spots.append(tuple(where))
    return values.at[spots[0]].set(smallest).at[spots[1]].set(top_value)


def block_levels(stream_key, extent, pieces, least, top_value):
    level, own = 1.0, jax.random.fold_in(stream_key, 6)
    for dim, blocks in pieces:
        heights = jnp.exp(jax.random.uniform(jax.random.fold_in(own, dim), (blocks,), jnp.float32, least / len(pieces), top_value / len(pieces)))
        level = level * jnp.repeat(heights, extent[dim] // blocks).reshape([-1 if axis == dim else 1 for axis in range(len(extent))])
    return level


def centred(stream_key, shape, scale, reach, split=(), kind=jnp.bfloat16):
    factor_of = block_levels(stream_key, shape, split, -0.22, 0.18) if split else 1.0
    drawn = jax.random.normal(stream_key, shape, jnp.float32) * scale * factor_of
    return jnp.minimum(jnp.maximum(drawn, -reach), reach).astype(kind)


def setup_inputs(seed: int = 0) -> dict:
    key_list = jax.random.split(jax.random.key(seed), 12)
    return {
        "encoded": centred(key_list[0], (SLABS, SAMP, RAYS, ENC), 1.0, 6.0, ((0, 16), (2, 8))),
        "spacing": jnp.clip(jnp.exp(math.log(0.05) - 3.218876 * jax.random.uniform(key_list[1], (SLABS, SAMP, RAYS), jnp.float32) ** block_levels(key_list[1], (SLABS, SAMP, RAYS), ((0, 16), (2, 8)), -0.2, 0.2)), 0.002, 0.05),
        "counts": set_ends(jax.random.randint(key_list[2], (SLABS, RAYS), 1, SAMP + 1), jax.random.fold_in(key_list[2], 1), 1, SAMP).astype(jnp.int32),
        "seg_first": set_ends(jax.random.randint(key_list[3], (RAYS,), 0, N_SLAB // 4), jax.random.fold_in(key_list[3], 1), 0, (N_SLAB // 4) - 1).astype(jnp.int32),
        "seg_last": set_ends(jax.random.randint(key_list[4], (RAYS,), N_SLAB - N_SLAB // 4 + 1, N_SLAB + 1), jax.random.fold_in(key_list[4], 1), N_SLAB - N_SLAB // 4 + 1, N_SLAB).astype(jnp.int32),
        "direction": set_ends(jax.random.randint(key_list[5], (RAYS,), 0, 2), jax.random.fold_in(key_list[5], 1), 0, 1).astype(jnp.int32),
        "field_in": centred(key_list[6], (SLABS, ENC, HID), ENC ** -0.5, 0.5, ((0, 16),)),
        "field_mid": centred(key_list[7], (SLABS, HID, HID), HID ** -0.5, 0.375, ((0, 16),)),
        "field_out": centred(key_list[8], (SLABS, HID, OUT), HID ** -0.5, 0.375, ((0, 16),)),
        "color_head": centred(key_list[9], (OUT, 3), OUT ** -0.5, 0.75, (), jnp.float32),
        "target": jnp.clip(1.0 * jax.random.uniform(key_list[10], (RAYS, 3), jnp.float32) ** block_levels(key_list[10], (RAYS, 3), ((0, 8),), -0.2, 0.2), 0.0, 1.0),
    }


def field(field_in, field_mid, field_out, inputs):
    hidden_one = jax.nn.relu(jnp.dot(inputs, field_in, preferred_element_type=jnp.float32)).astype(jnp.bfloat16)
    hidden_two = jax.nn.relu(jnp.dot(hidden_one, field_mid, preferred_element_type=jnp.float32)).astype(jnp.bfloat16)
    outputs = jnp.dot(hidden_two, field_out, preferred_element_type=jnp.float32)
    return (hidden_one, hidden_two, outputs)

def composite(outputs, spacing, live_mask, direction):
    optical = jax.nn.softplus(outputs[:, :, 0]) * spacing * live_mask
    running = jnp.cumsum(optical, axis=0)
    column_sum = running[-1]
    before = jnp.where(direction[None, :] > 0, column_sum[None, :] - running, running - optical)
    weights = jnp.exp(-before) * (1.0 - jnp.exp(-optical))
    colors = lax.optimization_barrier(jnp.sum(weights[:, :, None] * outputs, axis=0))
    return (jnp.exp(-column_sum), colors)

def make_combine(front_first):

    def combine(earlier, later):
        trans_early, color_early = earlier
        trans_late, color_late = later
        joined = jnp.where(front_first[:, None], color_early + trans_early[:, None] * color_late, color_late + trans_late[:, None] * color_early)
        return (trans_early * trans_late, joined)
    return combine

def field_grads(field_mid, field_out, inputs, hidden_one, hidden_two, grad_outputs):
    grad_low = grad_outputs.astype(jnp.bfloat16)
    grad_three = jnp.dot(hidden_two.T, grad_low, preferred_element_type=jnp.float32)
    back_two = (jnp.dot(grad_low, field_out.T, preferred_element_type=jnp.float32) * (hidden_two > 0)).astype(jnp.bfloat16)
    grad_two = jnp.dot(hidden_one.T, back_two, preferred_element_type=jnp.float32)
    back_one = (jnp.dot(back_two, field_mid.T, preferred_element_type=jnp.float32) * (hidden_one > 0)).astype(jnp.bfloat16)
    grad_one = jnp.dot(inputs.T, back_one, preferred_element_type=jnp.float32)
    return (grad_one, grad_two, grad_three)

def pixel_grad(color_total, color_head, target):
    logits = jnp.dot(color_total, color_head, precision=lax.Precision.HIGHEST)
    shade = jax.nn.sigmoid(logits)
    error = (shade - target) / RAYS_DEV
    return jnp.dot(error * shade * (1.0 - shade), color_head.T, precision=lax.Precision.HIGHEST)

def reference(encoded, spacing, counts, seg_first, seg_last, direction, field_in, field_mid, field_out, color_head, target):
    slab_ids = jnp.arange(N_SLAB, dtype=jnp.int32)
    sample_ids = jnp.arange(SAMP, dtype=jnp.int32)
    reverse_rays = direction > 0

    def live_of(slab):
        active = (seg_first <= slab) & (slab < seg_last)
        return ((sample_ids[:, None] < counts[slab][None, :]) & active[None, :]).astype(jnp.float32)

    def forward(slab):
        inputs = encoded[slab].reshape(-1, ENC)
        _, _, outputs = field(field_in[slab], field_mid[slab], field_out[slab], inputs)
        return composite(outputs.reshape(SAMP, -1, OUT), spacing[slab], live_of(slab), direction)
    seg_trans, seg_color = lax.map(forward, slab_ids)
    combine_low = make_combine(jnp.logical_not(reverse_rays))
    combine_high = make_combine(reverse_rays)
    identity = (jnp.ones((RAYS,), jnp.float32), jnp.zeros((RAYS, OUT), jnp.float32))

    def step_low(running_pair, item):
        return (combine_low(running_pair, item), running_pair)

    def step_high(running_pair, item):
        return (combine_high(running_pair, item), running_pair)
    final_pair, low_pairs = lax.scan(step_low, identity, (seg_trans, seg_color))
    _, high_pairs = lax.scan(step_high, identity, (seg_trans, seg_color), reverse=True)
    grad_color = pixel_grad(final_pair[1], color_head, target)
    front_trans = jnp.where(reverse_rays[None, :], high_pairs[0], low_pairs[0])
    back_color = jnp.where(reverse_rays[None, :, None], low_pairs[1], high_pairs[1])

    def backward(slab):
        inputs = encoded[slab].reshape(-1, ENC)
        hidden_one, hidden_two, outputs = field(field_in[slab], field_mid[slab], field_out[slab], inputs)
        live_mask = live_of(slab)
        space_here = spacing[slab]
        front_here = front_trans[slab]
        grad_seg_color = front_here[:, None] * grad_color
        grad_seg_trans = front_here * lax.optimization_barrier(jnp.sum(grad_color * back_color[slab], axis=1))
        _, pull_back = jax.vjp(lambda values: composite(values, space_here, live_mask, direction), outputs.reshape(SAMP, -1, OUT))
        grad_outputs = pull_back((grad_seg_trans, grad_seg_color))[0].reshape(-1, OUT)
        return field_grads(field_mid[slab], field_out[slab], inputs, hidden_one, hidden_two, grad_outputs)
    grad_in, grad_mid, grad_out = lax.map(backward, slab_ids)
    return (front_trans, grad_in, grad_mid, grad_out)
```

```python
import functools

import jax
import jax.numpy as jnp
from jax import lax
from jax.experimental import pallas as pl
from jax.experimental.pallas import tpu as pltpu
from jax.sharding import PartitionSpec as P

MESH = pl.DeviceIdType.MESH
NN = ((1,), (0,))
NT = ((1,), (1,))
LANES = 128


def mm(a, b, dims):
    return lax.dot_general(a, b, (dims, ((), ())), preferred_element_type=jnp.float32)


def running_sum(values):
    rows = values.shape[0]
    row_ids = lax.broadcasted_iota(jnp.int32, values.shape, 0)
    shift = 1
    while shift < rows:
        moved = pltpu.roll(values, shift, axis=0)
        values = values + jnp.where(row_ids >= shift, moved, 0.0)
        shift *= 2
    return values


def kernel(
    chunks,
    n_slab,
    n_tile,
    x_hbm,
    space_hbm,
    counts_hbm,
    first_hbm,
    last_hbm,
    dir_hbm,
    w1_hbm,
    w2_hbm,
    w3t_hbm,
    head_hbm,
    target_hbm,
    front_out,
    g1_out,
    g2_out,
    g3_out,
    x_s,
    space_s,
    ints_s,
    w1_s,
    w2_s,
    w3t_s,
    head_s,
    target_s,
    w1t_s,
    w2t_s,
    w3_s,
    head8_s,
    headt_s,
    w3p_s,
    h1_s,
    h2_s,
    b2_s,
    gl_s,
    proj_s,
    saved_s,
    row_s,
    send_s,
    gather_s,
    g1_s,
    g1t_s,
    g2_s,
    g3_s,
    half1_s,
    half2_s,
    half3_s,
    pair1_s,
    pair2_s,
    pair3_s,
    quad1_s,
    quad2_s,
    quad3_s,
    in_sem,
    ex_send,
    ex_recv,
    pair_send,
    pair_recv,
    quad_send,
    quad_recv,
    ag_send,
    ag_recv,
):
    samples, rays_dev = space_s.shape
    rays = rays_dev // chunks
    cols = samples * rays
    groups = rays // LANES
    me = lax.axis_index("slab")
    tile = lax.axis_index("tile")
    core, ypos = tile % 2, tile // 2
    n_y = n_tile // 2

    barrier = pltpu.get_barrier_semaphore()
    for step in range(1, n_slab):
        pl.semaphore_signal(
            barrier, inc=1, device_id={"slab": (me + step) % n_slab}, device_id_type=MESH
        )
    mates = [(ypos * 2 + 1 - core)] + [((ypos + d) % n_y) * 2 + core for d in range(1, n_y)]
    for mate in mates:
        pl.semaphore_signal(barrier, inc=1, device_id={"tile": mate}, device_id_type=MESH)

    small = [
        (w1_hbm.at[0], w1_s),
        (w2_hbm.at[0], w2_s),
        (w3t_hbm.at[0], w3t_s),
        (head_hbm, head_s),
        (space_hbm.at[0], space_s),
        (counts_hbm, ints_s.at[0]),
        (first_hbm, ints_s.at[1]),
        (last_hbm, ints_s.at[2]),
        (dir_hbm, ints_s.at[3]),
        (target_hbm, target_s),
    ]
    loads = [
        pltpu.make_async_copy(src, dst, in_sem.at[chunks + i]) for i, (src, dst) in enumerate(small)
    ]
    x_loads = [
        pltpu.make_async_copy(
            x_hbm.at[0, :, pl.ds(c * rays, rays), :], x_s.at[c], in_sem.at[c]
        )
        for c in range(chunks)
    ]
    loads[0].start()
    x_loads[0].start()
    for load in loads[1:]:
        load.start()
    for load in x_loads[1:]:
        load.start()

    loads[0].wait()
    w1t_s[...] = w1_s[...].T
    loads[1].wait()
    w2t_s[...] = w2_s[...].T
    loads[2].wait()
    w3_s[...] = w3t_s[...].T
    loads[3].wait()
    head8_s[...] = jnp.zeros_like(head8_s)
    lane = lax.broadcasted_iota(jnp.int32, (1, LANES), 1)
    head8_s[0:1, :] = (lane == 0).astype(jnp.float32)
    head8_s[1:4, 0 : head_s.shape[1]] = head_s[...]
    headt_s[...] = head8_s[...].T
    width = w3t_s.shape[0]
    folded = lax.dot_general(
        head8_s[:, 0:width],
        w3t_s[...].astype(jnp.float32),
        (NN, ((), ())),
        precision=lax.Precision.HIGHEST,
        preferred_element_type=jnp.float32,
    )
    hi = folded.astype(jnp.bfloat16)
    rest = folded - hi.astype(jnp.float32)
    mid = rest.astype(jnp.bfloat16)
    low = (rest - mid.astype(jnp.float32)).astype(jnp.bfloat16)
    w3p_s[...] = jnp.concatenate(
        [hi.astype(jnp.float32), mid.astype(jnp.float32), low.astype(jnp.float32), jnp.zeros_like(folded)],
        axis=0,
    ).astype(jnp.bfloat16)
    for load in loads[4:]:
        load.wait()

    row_ids = lax.broadcasted_iota(jnp.int32, (samples, rays), 0)
    tile_rows = lax.broadcasted_iota(jnp.int32, (8, LANES), 0)
    is_trans = (tile_rows % 4) == 0
    identity = is_trans.astype(jnp.float32)

    def spread(v):
        return jnp.where(tile_rows < 4, v[0:1, :], v[4:5, :])

    def ray_slice(c):
        return pl.ds(c * rays, rays)

    def exchange(c, step):
        peer = (me + step) % n_slab
        return pltpu.make_async_remote_copy(
            src_ref=send_s.at[c],
            dst_ref=gather_s.at[c, me],
            send_sem=ex_send.at[c, step],
            recv_sem=ex_recv.at[c, me],
            device_id={"slab": peer},
            device_id_type=MESH,
        )

    def forward(c):
        x_loads[c].wait()
        x = x_s[c].reshape(cols, x_s.shape[3])
        base = c * cols
        h1 = jnp.maximum(mm(w1t_s[...], x, NT).astype(jnp.bfloat16), 0)
        h1_s[:, pl.ds(base, cols)] = h1
        h2 = jnp.maximum(mm(w2t_s[...], h1, NN).astype(jnp.bfloat16), 0)
        h2_s[:, pl.ds(base, cols)] = h2
        p = mm(w3p_s[...], h2, NN)
        p = p[0:8, :] + (p[8:16, :] + p[16:24, :])
        for j in range(samples):
            for g in range(groups):
                at = j * rays + g * LANES
                proj_s[g, 8 * j : 8 * j + 8, :] = p[:, at : at + LANES]
        o0, *ps = (
            jnp.concatenate(
                [proj_s[g, pl.ds(k, samples, stride=8), :] for g in range(groups)], 1
            )
            for k in range(4)
        )
        rs = ray_slice(c)
        counts = ints_s[0, :, rs]
        first = ints_s[1, :, rs]
        last = ints_s[2, :, rs]
        reverse = ints_s[3, :, rs] > 0
        active = (first <= me) & (me < last)
        live = ((row_ids < counts) & active).astype(jnp.float32)
        span = space_s[:, rs] * live
        soft = jnp.maximum(o0, 0.0) + jnp.log1p(jnp.exp(-jnp.abs(o0)))
        optical = soft * span
        running = running_sum(optical)
        column = running[samples - 1 : samples, :]
        before = jnp.where(reverse, column - running, running - optical)
        gone = jnp.exp(-before)
        stay = jnp.exp(-optical)
        weights = gone * (1.0 - stay)
        trans = jnp.exp(-column)
        saved_s[c, 0] = weights
        saved_s[c, 1] = gone * stay
        saved_s[c, 2] = span * (1.0 / (1.0 + jnp.exp(-o0)))
        for k in range(3):
            saved_s[c, 3 + k] = ps[k]
        row_s[c] = trans
        rows = [trans] + [jnp.sum(weights * ps[k], axis=0, keepdims=True) for k in range(3)]
        for g in range(groups):
            for k in range(4):
                send_s[c, 4 * g + k : 4 * g + k + 1, :] = rows[k][:, g * LANES : (g + 1) * LANES]
        gather_s[c, me] = send_s[c]
        if c == 0:
            pl.semaphore_wait(barrier, n_slab - 1 + len(mates))
        for step in range(1, n_slab):
            exchange(c, step).start()

    def compose(c):
        for step in range(1, n_slab):
            source = (me + n_slab - step) % n_slab
            pltpu.make_async_remote_copy(
                src_ref=send_s.at[c],
                dst_ref=gather_s.at[c, source],
                send_sem=ex_send.at[c, step],
                recv_sem=ex_recv.at[c, source],
                device_id={"slab": source},
                device_id_type=MESH,
            ).wait_recv()
        rs = ray_slice(c)
        reverse = ints_s[3, :, rs] > 0
        rev = jnp.where(
            tile_rows < 4,
            jnp.broadcast_to(ints_s[3, :, pl.ds(c * rays, LANES)], (8, LANES)),
            jnp.broadcast_to(ints_s[3, :, pl.ds(c * rays + (groups - 1) * LANES, LANES)], (8, LANES)),
        ) > 0

        def step_of(run, item, item_first):
            run_t, item_t = spread(run), spread(item)
            run_first = jnp.where(is_trans, 0.0, run) + run_t * item
            late_first = jnp.where(is_trans, 0.0, item) + item_t * run
            return jnp.where(item_first, late_first, run_first)

        low = identity
        for s in range(n_slab):
            low = step_of(low, jnp.where(s < me, gather_s[c, s], identity), rev)
        high = identity
        for s in reversed(range(n_slab)):
            high = step_of(high, jnp.where(s > me, gather_s[c, s], identity), jnp.logical_not(rev))
        own = gather_s[c, me]
        front = jnp.where(rev, high, low)
        back = jnp.where(rev, low, high)
        front_t, own_t = spread(front), spread(own)
        logits = front + front_t * own + (front_t * own_t) * back
        shade = 1.0 / (1.0 + jnp.exp(-logits))
        target = jnp.zeros((8, LANES), jnp.float32)
        for g in range(groups):
            for k in range(3):
                target = jnp.where(
                    tile_rows == 4 * g + 1 + k,
                    target_s[k : k + 1, pl.ds(c * rays + g * LANES, LANES)],
                    target,
                )
        grad3 = jnp.where(is_trans, 0.0, (shade - target) * (1.0 / rays_dev) * shade * (1.0 - shade))
        dots = grad3 * back
        fronts, grads, seg_t = [], [[], [], []], []
        for g in range(groups):
            r = 4 * g
            fronts.append(front[r : r + 1, :])
            for k in range(3):
                grads[k].append(grad3[r + 1 + k : r + 2 + k, :])
            seg_t.append(dots[r + 1 : r + 2, :] + dots[r + 2 : r + 3, :] + dots[r + 3 : r + 4, :])
        join = lambda parts: jnp.concatenate(parts, 1)
        front_row = join(fronts)
        front_out[:, rs] = front_row
        grad_rows = [front_row * join(grads[k]) for k in range(3)]
        return reverse, grad_rows, front_row * join(seg_t)

    def backward(c):
        reverse, grad_rows, grad_trans = compose(c)
        weights, spent = saved_s[c, 0], saved_s[c, 1]
        grad_w = (
            grad_rows[0] * saved_s[c, 3] + grad_rows[1] * saved_s[c, 4] + grad_rows[2] * saved_s[c, 5]
        )
        pulled = weights * grad_w
        running = running_sum(pulled)
        total = running[samples - 1 : samples, :]
        later = jnp.where(reverse, running - pulled, total - running)
        grad_optical = spent * grad_w - row_s[c] * grad_trans - later
        grad_density = grad_optical * saved_s[c, 2]
        grad_color = (
            headt_s[0:width, 1:2] * grad_rows[0]
            + headt_s[0:width, 2:3] * grad_rows[1]
            + headt_s[0:width, 3:4] * grad_rows[2]
        )
        first_row = lax.broadcasted_iota(jnp.int32, (width, 1), 0) == 0
        base = c * cols
        for j in range(samples):
            at = pl.ds(base + j * rays, rays)
            gl_s[:, at] = (
                grad_color * weights[j : j + 1, :]
                + jnp.where(first_row, grad_density[j : j + 1, :], 0.0)
            ).astype(jnp.bfloat16)
        b2 = mm(w3_s[...], gl_s[:, pl.ds(base, cols)], NN).astype(jnp.bfloat16)
        b2 = jnp.where(h2_s[:, pl.ds(base, cols)] > 0, b2, 0)
        b2_s[:, pl.ds(base, cols)] = b2
        part = mm(h1_s[:, pl.ds(base, cols)], b2, NT)
        g2_s[...] = part if c == 0 else g2_s[...] + part

    def backward_one(c):
        base = c * cols
        b1 = mm(w2_s[...], b2_s[:, pl.ds(base, cols)], NN).astype(jnp.bfloat16)
        b1 = jnp.where(h1_s[:, pl.ds(base, cols)] > 0, b1, 0)
        part = mm(b1, x_s[c].reshape(cols, x_s.shape[3]), NN)
        g1t_s[...] = part if c == 0 else g1t_s[...] + part

    grads = (
        (g1_s, half1_s, pair1_s, quad1_s, g1_out),
        (g2_s, half2_s, pair2_s, quad2_s, g2_out),
        (g3_s, half3_s, pair3_s, quad3_s, g3_out),
    )

    def piece_rows(i, k, y):
        rows = grads[i][0].shape[0]
        return pl.ds(pl.multiple_of(k * (rows // 2) + y * (rows // n_tile), 8), rows // n_tile)

    def pair_copy(i):
        whole, half, pair = grads[i][:3]
        rows = half.shape[0]
        return pltpu.make_async_remote_copy(
            src_ref=whole.at[pl.ds(pl.multiple_of((1 - core) * rows, 8), rows), :],
            dst_ref=pair,
            send_sem=pair_send.at[i],
            recv_sem=pair_recv.at[i],
            device_id={"tile": ypos * 2 + 1 - core},
            device_id_type=MESH,
        )

    def pair_sum(i):
        whole, half, pair = grads[i][:3]
        rows = half.shape[0]
        pair_copy(i).wait_recv()
        half[...] = whole[pl.ds(pl.multiple_of(core * rows, 8), rows), :] + pair[...]

    def quad_copy(i, d):
        half, quad = grads[i][1], grads[i][3]
        rows = quad.shape[1]
        to = (ypos + d) % n_y
        return pltpu.make_async_remote_copy(
            src_ref=half.at[pl.ds(pl.multiple_of(to * rows, 8), rows), :],
            dst_ref=quad.at[d],
            send_sem=quad_send.at[i, d],
            recv_sem=quad_recv.at[i, d],
            device_id={"tile": to * 2 + core},
            device_id_type=MESH,
        )

    def quad_sum(i):
        half, quad, out = grads[i][1], grads[i][3], grads[i][4]
        rows = quad.shape[1]
        total = half[pl.ds(pl.multiple_of(ypos * rows, 8), rows), :]
        for d in range(1, n_y):
            quad_copy(i, d).wait_recv()
            total = total + quad[d]
        out[piece_rows(i, core, ypos), :] = total

    def gather_copy(i, y, to_tile, sem):
        out = grads[i][4]
        at = piece_rows(i, core, y)
        return pltpu.make_async_remote_copy(
            src_ref=out.at[at, :],
            dst_ref=out.at[at, :],
            send_sem=ag_send.at[i, sem],
            recv_sem=ag_recv.at[i, y * 2 + core],
            device_id={"tile": to_tile},
            device_id_type=MESH,
        )

    def gather_start(i):
        gather_copy(i, ypos, ypos * 2 + 1 - core, 0).start()
        for d in range(1, n_y):
            gather_copy(i, ypos, ((ypos + d) % n_y) * 2 + core, d).start()

    def gather_wait(i, k, y):
        out = grads[i][4]
        at = piece_rows(i, k, y)
        pltpu.make_async_remote_copy(
            src_ref=out.at[at, :],
            dst_ref=out.at[at, :],
            send_sem=ag_send.at[i, 0],
            recv_sem=ag_recv.at[i, y * 2 + k],
            device_id={"tile": ypos * 2 + 1 - core},
            device_id_type=MESH,
        ).wait_recv()

    def gather_forward(i):
        for d in range(1, n_y):
            y = (ypos + n_y - d) % n_y
            gather_wait(i, core, y)
            gather_copy(i, y, ypos * 2 + 1 - core, n_y - 1 + d).start()

    def gather_finish(i):
        for y in range(n_y):
            gather_wait(i, 1 - core, y)
        gather_copy(i, ypos, ypos * 2 + 1 - core, 0).wait_send()
        for d in range(1, n_y):
            gather_copy(i, ypos, ((ypos + d) % n_y) * 2 + core, d).wait_send()
            gather_copy(i, (ypos + n_y - d) % n_y, ypos * 2 + 1 - core, n_y - 1 + d).wait_send()
            quad_copy(i, d).wait_send()
        pair_copy(i).wait_send()

    def quad_start(i):
        for d in range(1, n_y):
            quad_copy(i, d).start()

    for c in range(chunks):
        forward(c)
    for c in range(chunks):
        backward(c)
    pair_copy(1).start()
    backward_one(0)
    pair_sum(1)
    quad_start(1)
    for c in range(1, chunks):
        backward_one(c)
    g1_s[...] = g1t_s[...].T
    pair_copy(0).start()
    quad_sum(1)
    gather_start(1)
    g3_s[...] = mm(gl_s[...], h2_s[...], NT)
    pair_copy(2).start()
    pair_sum(0)
    quad_start(0)
    gather_forward(1)
    pair_sum(2)
    quad_start(2)
    quad_sum(0)
    gather_start(0)
    quad_sum(2)
    gather_start(2)
    gather_forward(0)
    gather_forward(2)
    for i in (1, 0, 2):
        gather_finish(i)
    for c in range(chunks):
        for step in range(1, n_slab):
            exchange(c, step).wait_send()


def solution(mesh):
    n_slab, n_tile = mesh.shape["slab"], mesh.shape["tile"]
    chunks = 2

    def body(
        encoded,
        spacing,
        counts,
        seg_first,
        seg_last,
        direction,
        field_in,
        field_mid,
        field_out,
        color_head,
        target,
    ):
        _, samples, rays_dev, enc = encoded.shape
        hid, out = field_out.shape[1:]
        rays = rays_dev // chunks
        total = samples * rays_dev
        f32, bf16 = jnp.float32, jnp.bfloat16
        row = lambda v: v.reshape(1, rays_dev)
        sizes = ((enc, hid), (hid, hid), (out, hid))
        any_space = pl.BlockSpec(memory_space=pl.ANY)
        vmem = pl.BlockSpec(memory_space=pltpu.VMEM)
        scratch = [
            pltpu.VMEM((chunks, samples, rays, enc), bf16),
            pltpu.VMEM((samples, rays_dev), f32),
            pltpu.VMEM((4, 1, rays_dev), jnp.int32),
            pltpu.VMEM((enc, hid), bf16),
            pltpu.VMEM((hid, hid), bf16),
            pltpu.VMEM((out, hid), bf16),
            pltpu.VMEM((3, out), f32),
            pltpu.VMEM((3, rays_dev), f32),
            pltpu.VMEM((hid, enc), bf16),
            pltpu.VMEM((hid, hid), bf16),
            pltpu.VMEM((hid, out), bf16),
            pltpu.VMEM((8, LANES), f32),
            pltpu.VMEM((LANES, 8), f32),
            pltpu.VMEM((32, hid), bf16),
            pltpu.VMEM((hid, total), bf16),
            pltpu.VMEM((hid, total), bf16),
            pltpu.VMEM((hid, total), bf16),
            pltpu.VMEM((out, total), bf16),
            pltpu.VMEM((rays // LANES, 8 * samples, LANES), f32),
            pltpu.VMEM((chunks, 6, samples, rays), f32),
            pltpu.VMEM((chunks, 1, rays), f32),
            pltpu.VMEM((chunks, 8, LANES), f32),
            pltpu.VMEM((chunks, n_slab, 8, LANES), f32),
            pltpu.VMEM((enc, hid), f32),
            pltpu.VMEM((hid, enc), f32),
            pltpu.VMEM((hid, hid), f32),
            pltpu.VMEM((out, hid), f32),
            *(pltpu.VMEM((r // 2, n), f32) for r, n in sizes),
            *(pltpu.VMEM((r // 2, n), f32) for r, n in sizes),
            *(pltpu.VMEM((n_tile // 2, r // n_tile, n), f32) for r, n in sizes),
            pltpu.SemaphoreType.DMA((chunks + 10,)),
            pltpu.SemaphoreType.DMA((chunks, n_slab)),
            pltpu.SemaphoreType.DMA((chunks, n_slab)),
            pltpu.SemaphoreType.DMA((3,)),
            pltpu.SemaphoreType.DMA((3,)),
            pltpu.SemaphoreType.DMA((3, n_tile // 2)),
            pltpu.SemaphoreType.DMA((3, n_tile // 2)),
            pltpu.SemaphoreType.DMA((3, n_tile)),
            pltpu.SemaphoreType.DMA((3, n_tile)),
        ]
        front, g1, g2, g3t = pl.pallas_call(
            functools.partial(kernel, chunks, n_slab, n_tile),
            out_shape=(
                jax.ShapeDtypeStruct((1, rays_dev), f32),
                jax.ShapeDtypeStruct((enc, hid), f32),
                jax.ShapeDtypeStruct((hid, hid), f32),
                jax.ShapeDtypeStruct((out, hid), f32),
            ),
            in_specs=[any_space] * 11,
            out_specs=(vmem,) * 4,
            scratch_shapes=scratch,
            compiler_params=pltpu.CompilerParams(
                collective_id=0, has_side_effects=True, vmem_limit_bytes=56 * 2**20
            ),
        )(
            encoded,
            spacing,
            counts,
            row(seg_first),
            row(seg_last),
            row(direction),
            field_in,
            field_mid,
            field_out.transpose(0, 2, 1),
            color_head.T,
            target.T,
        )
        return front, g1[None], g2[None], g3t.T[None]

    return jax.shard_map(
        body,
        mesh=mesh,
        in_specs=(
            P("slab", None, "tile", None),
            P("slab", None, "tile"),
            P("slab", "tile"),
            P("tile"),
            P("tile"),
            P("tile"),
            P("slab", None, None),
            P("slab", None, None),
            P("slab", None, None),
            P(),
            P("tile", None),
        ),
        out_specs=(
            P("slab", "tile"),
            P("slab", None, None),
            P("slab", None, None),
            P("slab", None, None),
        ),
        check_vma=False,
    )
```

```python
import functools

import jax
import jax.numpy as jnp
from jax import lax
from jax.experimental import pallas as pl
from jax.experimental.pallas import tpu as pltpu
from jax.sharding import PartitionSpec as P

MESH = pl.DeviceIdType.MESH
NN = ((1,), (0,))
NT = ((1,), (1,))
LANES = 128


def mm(a, b, dims):
    return lax.dot_general(a, b, (dims, ((), ())), preferred_element_type=jnp.float32)


def running_sum(values):
    rows = values.shape[0]
    row_ids = lax.broadcasted_iota(jnp.int32, values.shape, 0)
    shift = 1
    while shift < rows:
        moved = pltpu.roll(values, shift, axis=0)
        values = values + jnp.where(row_ids >= shift, moved, 0.0)
        shift *= 2
    return values


def kernel(
    chunks,
    n_slab,
    n_tile,
    x_hbm,
    space_hbm,
    counts_hbm,
    first_hbm,
    last_hbm,
    dir_hbm,
    w1_hbm,
    w2_hbm,
    w3t_hbm,
    head_hbm,
    target_hbm,
    front_out,
    g1_out,
    g2_out,
    g3_out,
    x_s,
    space_s,
    ints_s,
    w1_s,
    w2_s,
    w3t_s,
    head_s,
    target_s,
    w1t_s,
    w2t_s,
    head8_s,
    headt_s,
    w3p_s,
    fold_s,
    foldt_s,
    h1_s,
    h2_s,
    b2_s,
    coef_s,
    proj_s,
    stack_s,
    saved_s,
    held_s,
    send_s,
    gather_s,
    g1_s,
    g1t_s,
    g2_s,
    g3_s,
    pair1_s,
    pair2_s,
    pair3_s,
    quad1_s,
    quad2_s,
    quad3_s,
    in_sem,
    ex_send,
    ex_recv,
    pair_send,
    pair_recv,
    quad_send,
    quad_recv,
    pass_send,
    pass_recv,
):
    samples, rays_dev = space_s.shape
    rays = rays_dev // chunks
    cols = samples * rays
    groups = rays // LANES
    me = lax.axis_index("slab")
    tile = lax.axis_index("tile")
    core, ypos = tile % 2, tile // 2
    n_y = n_tile // 2

    barrier = pltpu.get_barrier_semaphore()
    for step in range(1, n_slab):
        pl.semaphore_signal(
            barrier, inc=1, device_id={"slab": (me + step) % n_slab}, device_id_type=MESH
        )
    mates = [(ypos * 2 + 1 - core)] + [((ypos + d) % n_y) * 2 + core for d in range(1, n_y)]
    for mate in mates:
        pl.semaphore_signal(barrier, inc=1, device_id={"tile": mate}, device_id_type=MESH)

    small = [
        (w1_hbm.at[0], w1_s),
        (w2_hbm.at[0], w2_s),
        (w3t_hbm.at[0], w3t_s),
        (head_hbm, head_s),
        (space_hbm.at[0], space_s),
        (counts_hbm, ints_s.at[0]),
        (first_hbm, ints_s.at[1]),
        (last_hbm, ints_s.at[2]),
        (dir_hbm, ints_s.at[3]),
        (target_hbm, target_s),
    ]
    loads = [
        pltpu.make_async_copy(src, dst, in_sem.at[chunks + i]) for i, (src, dst) in enumerate(small)
    ]
    x_loads = [
        pltpu.make_async_copy(
            x_hbm.at[0, :, pl.ds(c * rays, rays), :], x_s.at[c], in_sem.at[c]
        )
        for c in range(chunks)
    ]
    loads[0].start()
    x_loads[0].start()
    for load in loads[1:]:
        load.start()
    for load in x_loads[1:]:
        load.start()

    loads[0].wait()
    w1t_s[...] = w1_s[...].T
    loads[1].wait()
    w2t_s[...] = w2_s[...].T
    loads[2].wait()
    loads[3].wait()
    head8_s[...] = jnp.zeros_like(head8_s)
    lane = lax.broadcasted_iota(jnp.int32, (1, LANES), 1)
    head8_s[0:1, :] = (lane == 0).astype(jnp.float32)
    head8_s[1:4, 0 : head_s.shape[1]] = head_s[...]
    headt_s[...] = head8_s[...].T
    width = w3t_s.shape[0]
    folded = lax.dot_general(
        head8_s[:, 0:width],
        w3t_s[...].astype(jnp.float32),
        (NN, ((), ())),
        precision=lax.Precision.HIGHEST,
        preferred_element_type=jnp.float32,
    )
    hi = folded.astype(jnp.bfloat16).astype(jnp.float32)
    mid = (folded - hi).astype(jnp.bfloat16).astype(jnp.float32)
    low = folded - hi - mid
    zeros = jnp.zeros_like(folded)
    w3p_s[...] = jnp.concatenate([hi, mid, low, zeros], axis=0).astype(jnp.bfloat16)
    fold_s[...] = jnp.zeros_like(fold_s)
    fold_s[0:4, :] = hi[0:4]
    fold_s[4:8, :] = hi[0:4]
    fold_s[8:12, :] = mid[0:4]
    foldt_s[...] = fold_s[...].T[:, 0:16].astype(jnp.bfloat16)
    stack_s[...] = jnp.zeros_like(stack_s)
    for load in loads[4:]:
        load.wait()

    row_ids = lax.broadcasted_iota(jnp.int32, (samples, rays), 0)
    tile_rows = lax.broadcasted_iota(jnp.int32, (8, LANES), 0)
    is_trans = (tile_rows % 4) == 0
    identity = is_trans.astype(jnp.float32)

    def spread(v):
        return jnp.where(tile_rows < 4, v[0:1, :], v[4:5, :])

    def ray_slice(c):
        return pl.ds(c * rays, rays)

    def exchange(step, source):
        return pltpu.make_async_remote_copy(
            src_ref=send_s,
            dst_ref=gather_s.at[source],
            send_sem=ex_send.at[step],
            recv_sem=ex_recv.at[source],
            device_id={"slab": (me + step) % n_slab},
            device_id_type=MESH,
        )

    def lanes_of(values, g):
        return values[:, g * LANES : (g + 1) * LANES]

    def later_sum(values, reverse):
        running = running_sum(values)
        return jnp.where(reverse, running - values, running[samples - 1 : samples, :] - running)

    def forward(c):
        x_loads[c].wait()
        x = x_s[c].reshape(cols, x_s.shape[3])
        base = c * cols
        h1 = jnp.maximum(mm(w1t_s[...], x, NT).astype(jnp.bfloat16), 0)
        h1_s[:, pl.ds(base, cols)] = h1
        h2 = jnp.maximum(mm(w2t_s[...], h1, NN).astype(jnp.bfloat16), 0)
        h2_s[:, pl.ds(base, cols)] = h2
        p = mm(w3p_s[...], h2, NN)
        p = p[0:8, :] + (p[8:16, :] + p[16:24, :])
        for j in range(samples):
            for g in range(groups):
                at = j * rays + g * LANES
                proj_s[c, g, 8 * j : 8 * j + 8, :] = p[:, at : at + LANES]
        o0, *ps = (
            jnp.concatenate(
                [proj_s[c, g, pl.ds(k, samples, stride=8), :] for g in range(groups)], 1
            )
            for k in range(4)
        )
        rs = ray_slice(c)
        counts = ints_s[0, :, rs]
        first = ints_s[1, :, rs]
        last = ints_s[2, :, rs]
        reverse = ints_s[3, :, rs] > 0
        active = (first <= me) & (me < last)
        live = ((row_ids < counts) & active).astype(jnp.float32)
        span = space_s[:, rs] * live
        soft = jnp.maximum(o0, 0.0) + jnp.log1p(jnp.exp(-jnp.abs(o0)))
        optical = soft * span
        running = running_sum(optical)
        column = running[samples - 1 : samples, :]
        before = jnp.where(reverse, column - running, running - optical)
        gone = jnp.exp(-before)
        stay = jnp.exp(-optical)
        weights = gone * (1.0 - stay)
        trans = jnp.exp(-column)
        shown = [weights * ps[k] for k in range(3)]
        rows = [trans] + [jnp.sum(shown[k], axis=0, keepdims=True) for k in range(3)]
        for g in range(groups):
            for k in range(4):
                send_s[c, 4 * g + k : 4 * g + k + 1, :] = lanes_of(rows[k], g)
        slope = span * (1.0 / (1.0 + jnp.exp(-o0)))
        spent = gone * stay
        saved_s[c, 0] = weights
        for k in range(3):
            saved_s[c, 1 + k] = slope * (spent * ps[k] - later_sum(shown[k], reverse))
        saved_s[c, 4] = -(trans * slope)

    def hold(c):
        base = c * cols
        block = 32
        for f in range(0, h2_s.shape[0], block):
            sums = [None] * 5
            for j in range(samples):
                h2 = h2_s[f : f + block, pl.ds(base + j * rays, rays)].astype(jnp.float32)
                for m in range(5):
                    term = h2 * saved_s[c, m, j : j + 1, :]
                    sums[m] = term if j == 0 else sums[m] + term
            for m in range(5):
                held_s[c, m, f : f + block, :] = sums[m]

    def compose(c):
        rs = ray_slice(c)
        rev = jnp.where(
            tile_rows < 4,
            jnp.broadcast_to(ints_s[3, :, pl.ds(c * rays, LANES)], (8, LANES)),
            jnp.broadcast_to(ints_s[3, :, pl.ds(c * rays + (groups - 1) * LANES, LANES)], (8, LANES)),
        ) > 0

        def step_of(run, item, item_first):
            run_t, item_t = spread(run), spread(item)
            run_first = jnp.where(is_trans, 0.0, run) + run_t * item
            late_first = jnp.where(is_trans, 0.0, item) + item_t * run
            return jnp.where(item_first, late_first, run_first)

        low = high = identity
        for s in range(n_slab):
            t = n_slab - 1 - s
            low = step_of(low, jnp.where(s < me, gather_s[s, c], identity), rev)
            high = step_of(high, jnp.where(t > me, gather_s[t, c], identity), jnp.logical_not(rev))
        own = send_s[c]
        front = jnp.where(rev, high, low)
        back = jnp.where(rev, low, high)
        front_t, own_t = spread(front), spread(own)
        logits = front + front_t * own + (front_t * own_t) * back
        shade = 1.0 / (1.0 + jnp.exp(-logits))
        target = jnp.zeros((8, LANES), jnp.float32)
        for g in range(groups):
            for k in range(3):
                target = jnp.where(
                    tile_rows == 4 * g + 1 + k,
                    target_s[k : k + 1, pl.ds(c * rays + g * LANES, LANES)],
                    target,
                )
        grad3 = jnp.where(is_trans, 0.0, (shade - target) * (1.0 / rays_dev) * shade * (1.0 - shade))
        seg = front_t * grad3
        dots = seg * back
        fronts, grads, seg_t = [], [[], [], []], []
        for g in range(groups):
            r = 4 * g
            fronts.append(front[r : r + 1, :])
            for k in range(3):
                grads[k].append(seg[r + 1 + k : r + 2 + k, :])
            seg_t.append(dots[r + 1 : r + 2, :] + dots[r + 2 : r + 3, :] + dots[r + 3 : r + 4, :])
        join = lambda parts: jnp.concatenate(parts, 1)
        front_out[:, rs] = join(fronts)
        return [join(grads[k]) for k in range(3)] + [join(seg_t)]

    def coefficients(c, cot):
        weights = saved_s[c, 0]
        density = (
            cot[0] * saved_s[c, 1] + cot[1] * saved_s[c, 2] + cot[2] * saved_s[c, 3] + cot[3] * saved_s[c, 4]
        )
        for m, value in enumerate([density] + [cot[k] * weights for k in range(3)]):
            hi = value.astype(jnp.bfloat16).astype(jnp.float32)
            for g in range(groups):
                for row, part in ((m, hi), (4 + m, value - hi), (8 + m, hi)):
                    stack_s[c, g, row * samples : (row + 1) * samples, :] = lanes_of(part, g)
        for j in range(samples):
            for g in range(groups):
                coef_s[:, pl.ds(c * cols + j * rays + g * LANES, LANES)] = jnp.concatenate(
                    [
                        stack_s[c, g, pl.ds(j, 8, stride=samples), :],
                        stack_s[c, g, pl.ds(8 * samples + j, 8, stride=samples), :],
                    ],
                    0,
                ).astype(jnp.bfloat16)

    def grad_out(cots):
        hid = h2_s.shape[0]
        block = 32
        column = lax.broadcasted_iota(jnp.int32, (block, LANES), 1)
        for f in range(0, hid, block):
            parts = [0.0] * 4
            for c in range(chunks):
                for g in range(groups):
                    at = pl.ds(g * LANES, LANES)
                    shown = held_s[c, 0, f : f + block, at]
                    for k in range(3):
                        parts[k] = parts[k] + shown * lanes_of(cots[c][k], g)
                    for m in range(4):
                        parts[3] = parts[3] + held_s[c, 1 + m, f : f + block, at] * lanes_of(cots[c][m], g)
            packed = jnp.zeros((block, LANES), jnp.float32)
            for k in range(4):
                packed = jnp.where(column == k, jnp.sum(parts[k], axis=1, keepdims=True), packed)
            held_s[0, 0, f : f + block, 0:LANES] = packed
        sums = held_s[0, 0, :, 0:LANES].T
        first_row = lax.broadcasted_iota(jnp.int32, (width, 1), 0) == 0
        total = jnp.where(first_row, sums[3:4, :], 0.0)
        for k in range(3):
            total = total + headt_s[0:width, 1 + k : 2 + k] * sums[k : k + 1, :]
        g3_s[...] = total

    def backward_two(c):
        base = c * cols
        b2 = mm(foldt_s[...], coef_s[:, pl.ds(base, cols)], NN).astype(jnp.bfloat16)
        b2 = jnp.where(h2_s[:, pl.ds(base, cols)] > 0, b2, 0)
        b2_s[:, pl.ds(base, cols)] = b2
        part = mm(h1_s[:, pl.ds(base, cols)], b2, NT)
        g2_s[...] = part if c == 0 else g2_s[...] + part

    def backward_one(c):
        base = c * cols
        b1 = mm(w2_s[...], b2_s[:, pl.ds(base, cols)], NN).astype(jnp.bfloat16)
        b1 = jnp.where(h1_s[:, pl.ds(base, cols)] > 0, b1, 0)
        part = mm(b1, x_s[c].reshape(cols, x_s.shape[3]), NN)
        g1t_s[...] = part if c == 0 else g1t_s[...] + part

    grads = (
        (g1_s, pair1_s, quad1_s, g1_out),
        (g2_s, pair2_s, quad2_s, g2_out),
        (g3_s, pair3_s, quad3_s, g3_out),
    )
    partner = ypos * 2 + 1 - core

    def half_rows(i, k):
        rows = grads[i][1].shape[0]
        return pl.ds(pl.multiple_of(k * rows, 8), rows)

    def pair_copy(i):
        whole, pair = grads[i][:2]
        return pltpu.make_async_remote_copy(
            src_ref=whole.at[half_rows(i, 1 - core), :],
            dst_ref=pair,
            send_sem=pair_send.at[i],
            recv_sem=pair_recv.at[i],
            device_id={"tile": partner},
            device_id_type=MESH,
        )

    def quad_copy(i, d, source):
        quad = grads[i][2]
        return pltpu.make_async_remote_copy(
            src_ref=quad.at[ypos],
            dst_ref=quad.at[source],
            send_sem=quad_send.at[i, d],
            recv_sem=quad_recv.at[i, source],
            device_id={"tile": ((ypos + d) % n_y) * 2 + core},
            device_id_type=MESH,
        )

    def pass_copy(i, k):
        out = grads[i][3]
        at = half_rows(i, k)
        return pltpu.make_async_remote_copy(
            src_ref=out.at[at, :],
            dst_ref=out.at[at, :],
            send_sem=pass_send.at[i],
            recv_sem=pass_recv.at[i],
            device_id={"tile": partner},
            device_id_type=MESH,
        )

    def spread_half(i):
        whole, pair, quad = grads[i][:3]
        pair_copy(i).wait_recv()
        quad[ypos] = whole[half_rows(i, core), :] + pair[...]
        for d in range(1, n_y):
            quad_copy(i, d, ypos).start()

    def finish_half(i):
        quad, out = grads[i][2:]
        for d in range(1, n_y):
            quad_copy(i, d, (ypos + n_y - d) % n_y).wait_recv()
        total = quad[0]
        for y in range(1, n_y):
            total = total + quad[y]
        out[half_rows(i, core), :] = total
        pass_copy(i, core).start()

    for c in range(chunks):
        forward(c)
    pl.semaphore_wait(barrier, n_slab - 1 + len(mates))
    for step in range(1, n_slab):
        exchange(step, me).start()
    gather_s[me] = send_s[...]
    for c in range(chunks):
        hold(c)
    for step in range(1, n_slab):
        exchange(step, (me + n_slab - step) % n_slab).wait_recv()
    cots = [compose(c) for c in range(chunks)]
    for c in range(chunks):
        coefficients(c, cots[c])
    grad_out(cots)
    pair_copy(2).start()
    backward_two(0)
    spread_half(2)
    for c in range(1, chunks):
        backward_two(c)
    pair_copy(1).start()
    backward_one(0)
    spread_half(1)
    for c in range(1, chunks):
        backward_one(c)
    g1_s[...] = g1t_s[...].T
    pair_copy(0).start()
    finish_half(2)
    spread_half(0)
    finish_half(1)
    finish_half(0)
    for i in (2, 1, 0):
        pass_copy(i, 1 - core).wait_recv()
    for i in (2, 1, 0):
        pass_copy(i, core).wait_send()
        pair_copy(i).wait_send()
        for d in range(1, n_y):
            quad_copy(i, d, ypos).wait_send()
    for step in range(1, n_slab):
        exchange(step, me).wait_send()


def hand_on(*refs):
    half = len(refs) // 2
    sem = refs[-1]
    copies = [
        pltpu.make_async_copy(src, dst, sem.at[i])
        for i, (src, dst) in enumerate(zip(refs[:half], refs[half : 2 * half]))
    ]
    for copy in copies:
        copy.start()
    for copy in copies:
        copy.wait()


def solution(mesh):
    n_slab, n_tile = mesh.shape["slab"], mesh.shape["tile"]
    chunks = 2

    def body(
        encoded,
        spacing,
        counts,
        seg_first,
        seg_last,
        direction,
        field_in,
        field_mid,
        field_out,
        color_head,
        target,
    ):
        _, samples, rays_dev, enc = encoded.shape
        hid, out = field_out.shape[1:]
        rays = rays_dev // chunks
        total = samples * rays_dev
        f32, bf16 = jnp.float32, jnp.bfloat16
        row = lambda v: v.reshape(1, rays_dev)
        sizes = ((enc, hid), (hid, hid), (out, hid))
        any_space = pl.BlockSpec(memory_space=pl.ANY)
        vmem = pl.BlockSpec(memory_space=pltpu.VMEM)
        scratch = [
            pltpu.VMEM((chunks, samples, rays, enc), bf16),
            pltpu.VMEM((samples, rays_dev), f32),
            pltpu.VMEM((4, 1, rays_dev), jnp.int32),
            pltpu.VMEM((enc, hid), bf16),
            pltpu.VMEM((hid, hid), bf16),
            pltpu.VMEM((out, hid), bf16),
            pltpu.VMEM((3, out), f32),
            pltpu.VMEM((3, rays_dev), f32),
            pltpu.VMEM((hid, enc), bf16),
            pltpu.VMEM((hid, hid), bf16),
            pltpu.VMEM((8, LANES), f32),
            pltpu.VMEM((LANES, 8), f32),
            pltpu.VMEM((32, hid), bf16),
            pltpu.VMEM((LANES, hid), f32),
            pltpu.VMEM((hid, 16), bf16),
            pltpu.VMEM((hid, total), bf16),
            pltpu.VMEM((hid, total), bf16),
            pltpu.VMEM((hid, total), bf16),
            pltpu.VMEM((16, total), bf16),
            pltpu.VMEM((chunks, rays // LANES, 8 * samples, LANES), f32),
            pltpu.VMEM((chunks, rays // LANES, 16 * samples, LANES), f32),
            pltpu.VMEM((chunks, 5, samples, rays), f32),
            pltpu.VMEM((chunks, 5, hid, rays), f32),
            pltpu.VMEM((chunks, 8, LANES), f32),
            pltpu.VMEM((n_slab, chunks, 8, LANES), f32),
            pltpu.VMEM((enc, hid), f32),
            pltpu.VMEM((hid, enc), f32),
            pltpu.VMEM((hid, hid), f32),
            pltpu.VMEM((out, hid), f32),
            *(pltpu.VMEM((r // 2, n), f32) for r, n in sizes),
            *(pltpu.VMEM((n_tile // 2, r // 2, n), f32) for r, n in sizes),
            pltpu.SemaphoreType.DMA((chunks + 10,)),
            pltpu.SemaphoreType.DMA((n_slab,)),
            pltpu.SemaphoreType.DMA((n_slab,)),
            pltpu.SemaphoreType.DMA((3,)),
            pltpu.SemaphoreType.DMA((3,)),
            pltpu.SemaphoreType.DMA((3, n_tile // 2)),
            pltpu.SemaphoreType.DMA((3, n_tile // 2)),
            pltpu.SemaphoreType.DMA((3,)),
            pltpu.SemaphoreType.DMA((3,)),
        ]
        shapes = (
            jax.ShapeDtypeStruct((1, rays_dev), f32),
            jax.ShapeDtypeStruct((enc, hid), f32),
            jax.ShapeDtypeStruct((hid, hid), f32),
            jax.ShapeDtypeStruct((out, hid), f32),
        )
        results = pl.pallas_call(
            functools.partial(kernel, chunks, n_slab, n_tile),
            out_shape=shapes,
            in_specs=[any_space] * 11,
            out_specs=(vmem,) * 4,
            scratch_shapes=scratch,
            compiler_params=pltpu.CompilerParams(
                collective_id=0, has_side_effects=True, vmem_limit_bytes=56 * 2**20
            ),
        )(
            encoded,
            spacing,
            counts,
            row(seg_first),
            row(seg_last),
            row(direction),
            field_in,
            field_mid,
            field_out.transpose(0, 2, 1),
            color_head.T,
            target.T,
        )
        front, g1, g2, g3t = pl.pallas_call(
            hand_on,
            out_shape=shapes,
            in_specs=[any_space] * 4,
            out_specs=(any_space,) * 4,
            scratch_shapes=[pltpu.SemaphoreType.DMA((4,))],
        )(*results)
        return front, g1[None], g2[None], g3t.T[None]

    return jax.shard_map(
        body,
        mesh=mesh,
        in_specs=(
            P("slab", None, "tile", None),
            P("slab", None, "tile"),
            P("slab", "tile"),
            P("tile"),
            P("tile"),
            P("tile"),
            P("slab", None, None),
            P("slab", None, None),
            P("slab", None, None),
            P(),
            P("tile", None),
        ),
        out_specs=(
            P("slab", "tile"),
            P("slab", None, None),
            P("slab", None, None),
            P("slab", None, None),
        ),
        check_vma=False,
    )
```

```python
import functools

import jax
import jax.numpy as jnp
from jax import lax
from jax.experimental import pallas as pl
from jax.experimental.pallas import tpu as pltpu
from jax.sharding import PartitionSpec as P

MESH = pl.DeviceIdType.MESH
NN = ((1,), (0,))
NT = ((1,), (1,))
LANES = 128


def mm(a, b, dims):
    return lax.dot_general(a, b, (dims, ((), ())), preferred_element_type=jnp.float32)


def running_sum(values):
    rows = values.shape[0]
    row_ids = lax.broadcasted_iota(jnp.int32, values.shape, 0)
    shift = 1
    while shift < rows:
        moved = pltpu.roll(values, shift, axis=0)
        values = values + jnp.where(row_ids >= shift, moved, 0.0)
        shift *= 2
    return values


def kernel(
    chunks,
    n_slab,
    n_tile,
    x_hbm,
    space_hbm,
    counts_hbm,
    first_hbm,
    last_hbm,
    dir_hbm,
    w1_hbm,
    w2_hbm,
    w3t_hbm,
    head_hbm,
    target_hbm,
    front_out,
    g1_out,
    g2_out,
    g3_out,
    x_s,
    space_s,
    ints_s,
    w1_s,
    w2_s,
    w3t_s,
    head_s,
    target_s,
    w1t_s,
    w2t_s,
    head8_s,
    headt_s,
    w3p_s,
    fold_s,
    foldt_s,
    h1_s,
    h2_s,
    b2_s,
    coef_s,
    proj_s,
    stack_s,
    saved_s,
    held_s,
    send_s,
    gather_s,
    g1_s,
    g1t_s,
    g2_s,
    g3_s,
    pair1_s,
    pair2_s,
    pair3_s,
    quad1_s,
    quad2_s,
    quad3_s,
    in_sem,
    ex_send,
    ex_recv,
    pair_send,
    pair_recv,
    quad_send,
    quad_recv,
    pass_send,
    pass_recv,
):
    samples, rays_dev = space_s.shape
    rays = rays_dev // chunks
    cols = samples * rays
    groups = rays // LANES
    me = lax.axis_index("slab")
    tile = lax.axis_index("tile")
    core, ypos = tile % 2, tile // 2
    n_y = n_tile // 2

    barrier = pltpu.get_barrier_semaphore()
    for step in range(1, n_slab):
        pl.semaphore_signal(
            barrier, inc=1, device_id={"slab": (me + step) % n_slab}, device_id_type=MESH
        )
    mates = [(ypos * 2 + 1 - core)] + [((ypos + d) % n_y) * 2 + core for d in range(1, n_y)]
    for mate in mates:
        pl.semaphore_signal(barrier, inc=1, device_id={"tile": mate}, device_id_type=MESH)

    small = [
        (w1_hbm.at[0], w1_s),
        (w2_hbm.at[0], w2_s),
        (w3t_hbm.at[0], w3t_s),
        (head_hbm, head_s),
        (space_hbm.at[0], space_s),
        (counts_hbm, ints_s.at[0]),
        (first_hbm, ints_s.at[1]),
        (last_hbm, ints_s.at[2]),
        (dir_hbm, ints_s.at[3]),
        (target_hbm, target_s),
    ]
    loads = [
        pltpu.make_async_copy(src, dst, in_sem.at[chunks + i]) for i, (src, dst) in enumerate(small)
    ]
    x_loads = [
        pltpu.make_async_copy(
            x_hbm.at[0, :, pl.ds(c * rays, rays), :], x_s.at[c], in_sem.at[c]
        )
        for c in range(chunks)
    ]
    loads[0].start()
    x_loads[0].start()
    for load in loads[1:]:
        load.start()
    for load in x_loads[1:]:
        load.start()

    loads[0].wait()
    w1t_s[...] = w1_s[...].T
    loads[1].wait()
    w2t_s[...] = w2_s[...].T
    loads[2].wait()
    loads[3].wait()
    head8_s[...] = jnp.zeros_like(head8_s)
    lane = lax.broadcasted_iota(jnp.int32, (1, LANES), 1)
    head8_s[0:1, :] = (lane == 0).astype(jnp.float32)
    head8_s[1:4, 0 : head_s.shape[1]] = head_s[...]
    headt_s[...] = head8_s[...].T
    width = w3t_s.shape[0]
    folded = lax.dot_general(
        head8_s[:, 0:width],
        w3t_s[...].astype(jnp.float32),
        (NN, ((), ())),
        precision=lax.Precision.HIGHEST,
        preferred_element_type=jnp.float32,
    )
    hi = folded.astype(jnp.bfloat16).astype(jnp.float32)
    mid = (folded - hi).astype(jnp.bfloat16).astype(jnp.float32)
    low = folded - hi - mid
    zeros = jnp.zeros_like(folded)
    w3p_s[...] = jnp.concatenate([hi, mid, low, zeros], axis=0).astype(jnp.bfloat16)
    fold_s[...] = jnp.zeros_like(fold_s)
    fold_s[0:4, :] = hi[0:4]
    fold_s[4:8, :] = hi[0:4]
    fold_s[8:12, :] = mid[0:4]
    foldt_s[...] = fold_s[...].T[:, 0:16].astype(jnp.bfloat16)
    stack_s[...] = jnp.zeros_like(stack_s)
    for load in loads[4:]:
        load.wait()

    row_ids = lax.broadcasted_iota(jnp.int32, (samples, rays), 0)
    tile_rows = lax.broadcasted_iota(jnp.int32, (8, LANES), 0)
    is_trans = (tile_rows % 4) == 0
    identity = is_trans.astype(jnp.float32)

    def spread(v):
        return jnp.where(tile_rows < 4, v[0:1, :], v[4:5, :])

    def ray_slice(c):
        return pl.ds(c * rays, rays)

    def exchange(step, source):
        return pltpu.make_async_remote_copy(
            src_ref=send_s,
            dst_ref=gather_s.at[source],
            send_sem=ex_send.at[step],
            recv_sem=ex_recv.at[source],
            device_id={"slab": (me + step) % n_slab},
            device_id_type=MESH,
        )

    def lanes_of(values, g):
        return values[:, g * LANES : (g + 1) * LANES]

    def later_sum(values, reverse):
        running = running_sum(values)
        return jnp.where(reverse, running - values, running[samples - 1 : samples, :] - running)

    def forward(c):
        x_loads[c].wait()
        x = x_s[c].reshape(cols, x_s.shape[3])
        base = c * cols
        h1 = jnp.maximum(mm(w1t_s[...], x, NT).astype(jnp.bfloat16), 0)
        h1_s[:, pl.ds(base, cols)] = h1
        h2 = jnp.maximum(mm(w2t_s[...], h1, NN).astype(jnp.bfloat16), 0)
        h2_s[:, pl.ds(base, cols)] = h2
        p = mm(w3p_s[...], h2, NN)
        p = p[0:8, :] + (p[8:16, :] + p[16:24, :])
        for j in range(samples):
            for g in range(groups):
                at = j * rays + g * LANES
                proj_s[c, g, 8 * j : 8 * j + 8, :] = p[:, at : at + LANES]
        o0, *ps = (
            jnp.concatenate(
                [proj_s[c, g, pl.ds(k, samples, stride=8), :] for g in range(groups)], 1
            )
            for k in range(4)
        )
        rs = ray_slice(c)
        counts = ints_s[0, :, rs]
        first = ints_s[1, :, rs]
        last = ints_s[2, :, rs]
        reverse = ints_s[3, :, rs] > 0
        active = (first <= me) & (me < last)
        live = ((row_ids < counts) & active).astype(jnp.float32)
        span = space_s[:, rs] * live
        soft = jnp.maximum(o0, 0.0) + jnp.log1p(jnp.exp(-jnp.abs(o0)))
        optical = soft * span
        running = running_sum(optical)
        column = running[samples - 1 : samples, :]
        before = jnp.where(reverse, column - running, running - optical)
        gone = jnp.exp(-before)
        stay = jnp.exp(-optical)
        weights = gone * (1.0 - stay)
        trans = jnp.exp(-column)
        shown = [weights * ps[k] for k in range(3)]
        rows = [trans] + [jnp.sum(shown[k], axis=0, keepdims=True) for k in range(3)]
        for g in range(groups):
            for k in range(4):
                send_s[c, 4 * g + k : 4 * g + k + 1, :] = lanes_of(rows[k], g)
        slope = span * (1.0 / (1.0 + jnp.exp(-o0)))
        spent = gone * stay
        saved_s[c, 0] = weights
        for k in range(3):
            saved_s[c, 1 + k] = slope * (spent * ps[k] - later_sum(shown[k], reverse))
        saved_s[c, 4] = -(trans * slope)

    def hold(c):
        base = c * cols
        block = 32
        for f in range(0, h2_s.shape[0], block):
            sums = [None] * 5
            for j in range(samples):
                h2 = h2_s[f : f + block, pl.ds(base + j * rays, rays)].astype(jnp.float32)
                for m in range(5):
                    term = h2 * saved_s[c, m, j : j + 1, :]
                    sums[m] = term if j == 0 else sums[m] + term
            for m in range(5):
                held_s[c, m, f : f + block, :] = sums[m]

    def compose(c):
        rs = ray_slice(c)
        rev = jnp.where(
            tile_rows < 4,
            jnp.broadcast_to(ints_s[3, :, pl.ds(c * rays, LANES)], (8, LANES)),
            jnp.broadcast_to(ints_s[3, :, pl.ds(c * rays + (groups - 1) * LANES, LANES)], (8, LANES)),
        ) > 0

        def step_of(run, item, item_first):
            run_t, item_t = spread(run), spread(item)
            run_first = jnp.where(is_trans, 0.0, run) + run_t * item
            late_first = jnp.where(is_trans, 0.0, item) + item_t * run
            return jnp.where(item_first, late_first, run_first)

        low = high = identity
        for s in range(n_slab):
            t = n_slab - 1 - s
            low = step_of(low, jnp.where(s < me, gather_s[s, c], identity), rev)
            high = step_of(high, jnp.where(t > me, gather_s[t, c], identity), jnp.logical_not(rev))
        own = send_s[c]
        front = jnp.where(rev, high, low)
        back = jnp.where(rev, low, high)
        front_t, own_t = spread(front), spread(own)
        logits = front + front_t * own + (front_t * own_t) * back
        shade = 1.0 / (1.0 + jnp.exp(-logits))
        target = jnp.zeros((8, LANES), jnp.float32)
        for g in range(groups):
            for k in range(3):
                target = jnp.where(
                    tile_rows == 4 * g + 1 + k,
                    target_s[k : k + 1, pl.ds(c * rays + g * LANES, LANES)],
                    target,
                )
        grad3 = jnp.where(is_trans, 0.0, (shade - target) * (1.0 / rays_dev) * shade * (1.0 - shade))
        seg = front_t * grad3
        dots = seg * back
        fronts, grads, seg_t = [], [[], [], []], []
        for g in range(groups):
            r = 4 * g
            fronts.append(front[r : r + 1, :])
            for k in range(3):
                grads[k].append(seg[r + 1 + k : r + 2 + k, :])
            seg_t.append(dots[r + 1 : r + 2, :] + dots[r + 2 : r + 3, :] + dots[r + 3 : r + 4, :])
        join = lambda parts: jnp.concatenate(parts, 1)
        front_out[:, rs] = join(fronts)
        return [join(grads[k]) for k in range(3)] + [join(seg_t)]

    def coefficients(c, cot):
        weights = saved_s[c, 0]
        density = (
            cot[0] * saved_s[c, 1] + cot[1] * saved_s[c, 2] + cot[2] * saved_s[c, 3] + cot[3] * saved_s[c, 4]
        )
        for m, value in enumerate([density] + [cot[k] * weights for k in range(3)]):
            hi = value.astype(jnp.bfloat16).astype(jnp.float32)
            for g in range(groups):
                for row, part in ((m, hi), (4 + m, value - hi), (8 + m, hi)):
                    stack_s[c, g, row * samples : (row + 1) * samples, :] = lanes_of(part, g)
        for j in range(samples):
            for g in range(groups):
                coef_s[:, pl.ds(c * cols + j * rays + g * LANES, LANES)] = jnp.concatenate(
                    [
                        stack_s[c, g, pl.ds(j, 8, stride=samples), :],
                        stack_s[c, g, pl.ds(8 * samples + j, 8, stride=samples), :],
                    ],
                    0,
                ).astype(jnp.bfloat16)

    def grad_out(cots):
        hid = h2_s.shape[0]
        block = 32
        column = lax.broadcasted_iota(jnp.int32, (block, LANES), 1)
        for f in range(0, hid, block):
            parts = [0.0] * 4
            for c in range(chunks):
                for g in range(groups):
                    at = pl.ds(g * LANES, LANES)
                    shown = held_s[c, 0, f : f + block, at]
                    for k in range(3):
                        parts[k] = parts[k] + shown * lanes_of(cots[c][k], g)
                    for m in range(4):
                        parts[3] = parts[3] + held_s[c, 1 + m, f : f + block, at] * lanes_of(cots[c][m], g)
            packed = jnp.zeros((block, LANES), jnp.float32)
            for k in range(4):
                packed = jnp.where(column == k, jnp.sum(parts[k], axis=1, keepdims=True), packed)
            held_s[0, 0, f : f + block, 0:LANES] = packed
        sums = held_s[0, 0, :, 0:LANES].T
        first_row = lax.broadcasted_iota(jnp.int32, (width, 1), 0) == 0
        total = jnp.where(first_row, sums[3:4, :], 0.0)
        for k in range(3):
            total = total + headt_s[0:width, 1 + k : 2 + k] * sums[k : k + 1, :]
        g3_s[...] = total

    def backward_two(c):
        base = c * cols
        b2 = mm(foldt_s[...], coef_s[:, pl.ds(base, cols)], NN).astype(jnp.bfloat16)
        b2 = jnp.where(h2_s[:, pl.ds(base, cols)] > 0, b2, 0)
        b2_s[:, pl.ds(base, cols)] = b2
        part = mm(h1_s[:, pl.ds(base, cols)], b2, NT)
        g2_s[...] = part if c == 0 else g2_s[...] + part

    def backward_one(c):
        base = c * cols
        b1 = mm(w2_s[...], b2_s[:, pl.ds(base, cols)], NN).astype(jnp.bfloat16)
        b1 = jnp.where(h1_s[:, pl.ds(base, cols)] > 0, b1, 0)
        part = mm(b1, x_s[c].reshape(cols, x_s.shape[3]), NN)
        g1t_s[...] = part if c == 0 else g1t_s[...] + part

    grads = (
        (g1_s, pair1_s, quad1_s, g1_out),
        (g2_s, pair2_s, quad2_s, g2_out),
        (g3_s, pair3_s, quad3_s, g3_out),
    )
    partner = ypos * 2 + 1 - core

    def half_rows(i, k):
        rows = grads[i][1].shape[0]
        return pl.ds(pl.multiple_of(k * rows, 8), rows)

    def pair_copy(i):
        whole, pair = grads[i][:2]
        return pltpu.make_async_remote_copy(
            src_ref=whole.at[half_rows(i, 1 - core), :],
            dst_ref=pair,
            send_sem=pair_send.at[i],
            recv_sem=pair_recv.at[i],
            device_id={"tile": partner},
            device_id_type=MESH,
        )

    def quad_copy(i, d, source):
        quad = grads[i][2]
        return pltpu.make_async_remote_copy(
            src_ref=quad.at[ypos],
            dst_ref=quad.at[source],
            send_sem=quad_send.at[i, d],
            recv_sem=quad_recv.at[i, source],
            device_id={"tile": ((ypos + d) % n_y) * 2 + core},
            device_id_type=MESH,
        )

    def pass_copy(i, k):
        out = grads[i][3]
        at = half_rows(i, k)
        return pltpu.make_async_remote_copy(
            src_ref=out.at[at, :],
            dst_ref=out.at[at, :],
            send_sem=pass_send.at[i],
            recv_sem=pass_recv.at[i],
            device_id={"tile": partner},
            device_id_type=MESH,
        )

    def spread_half(i):
        whole, pair, quad = grads[i][:3]
        pair_copy(i).wait_recv()
        quad[ypos] = whole[half_rows(i, core), :] + pair[...]
        for d in range(1, n_y):
            quad_copy(i, d, ypos).start()

    def finish_half(i):
        quad, out = grads[i][2:]
        for d in range(1, n_y):
            quad_copy(i, d, (ypos + n_y - d) % n_y).wait_recv()
        total = quad[0]
        for y in range(1, n_y):
            total = total + quad[y]
        out[half_rows(i, core), :] = total
        pass_copy(i, core).start()

    for c in range(chunks):
        forward(c)
    pl.semaphore_wait(barrier, n_slab - 1 + len(mates))
    for step in range(1, n_slab):
        exchange(step, me).start()
    gather_s[me] = send_s[...]
    for c in range(chunks):
        hold(c)
    for step in range(1, n_slab):
        exchange(step, (me + n_slab - step) % n_slab).wait_recv()
    cots = [compose(c) for c in range(chunks)]
    for c in range(chunks):
        coefficients(c, cots[c])
    grad_out(cots)
    pair_copy(2).start()
    backward_two(0)
    spread_half(2)
    for c in range(1, chunks):
        backward_two(c)
    pair_copy(1).start()
    backward_one(0)
    spread_half(1)
    for c in range(1, chunks):
        backward_one(c)
    g1_s[...] = g1t_s[...].T
    pair_copy(0).start()
    finish_half(2)
    spread_half(0)
    finish_half(1)
    finish_half(0)
    for i in (2, 1, 0):
        pass_copy(i, 1 - core).wait_recv()
    for i in (2, 1, 0):
        pass_copy(i, core).wait_send()
        pair_copy(i).wait_send()
        for d in range(1, n_y):
            quad_copy(i, d, ypos).wait_send()
    for step in range(1, n_slab):
        exchange(step, me).wait_send()


def hand_on(*refs):
    half = len(refs) // 2
    for src, dst in zip(refs[:half], refs[half:]):
        dst[...] = src[...]


def solution(mesh):
    n_slab, n_tile = mesh.shape["slab"], mesh.shape["tile"]
    chunks = 2

    def body(
        encoded,
        spacing,
        counts,
        seg_first,
        seg_last,
        direction,
        field_in,
        field_mid,
        field_out,
        color_head,
        target,
    ):
        _, samples, rays_dev, enc = encoded.shape
        hid, out = field_out.shape[1:]
        rays = rays_dev // chunks
        total = samples * rays_dev
        f32, bf16 = jnp.float32, jnp.bfloat16
        row = lambda v: v.reshape(1, rays_dev)
        sizes = ((enc, hid), (hid, hid), (out, hid))
        any_space = pl.BlockSpec(memory_space=pl.ANY)
        vmem = pl.BlockSpec(memory_space=pltpu.VMEM)
        scratch = [
            pltpu.VMEM((chunks, samples, rays, enc), bf16),
            pltpu.VMEM((samples, rays_dev), f32),
            pltpu.VMEM((4, 1, rays_dev), jnp.int32),
            pltpu.VMEM((enc, hid), bf16),
            pltpu.VMEM((hid, hid), bf16),
            pltpu.VMEM((out, hid), bf16),
            pltpu.VMEM((3, out), f32),
            pltpu.VMEM((3, rays_dev), f32),
            pltpu.VMEM((hid, enc), bf16),
            pltpu.VMEM((hid, hid), bf16),
            pltpu.VMEM((8, LANES), f32),
            pltpu.VMEM((LANES, 8), f32),
            pltpu.VMEM((32, hid), bf16),
            pltpu.VMEM((LANES, hid), f32),
            pltpu.VMEM((hid, 16), bf16),
            pltpu.VMEM((hid, total), bf16),
            pltpu.VMEM((hid, total), bf16),
            pltpu.VMEM((hid, total), bf16),
            pltpu.VMEM((16, total), bf16),
            pltpu.VMEM((chunks, rays // LANES, 8 * samples, LANES), f32),
            pltpu.VMEM((chunks, rays // LANES, 16 * samples, LANES), f32),
            pltpu.VMEM((chunks, 5, samples, rays), f32),
            pltpu.VMEM((chunks, 5, hid, rays), f32),
            pltpu.VMEM((chunks, 8, LANES), f32),
            pltpu.VMEM((n_slab, chunks, 8, LANES), f32),
            pltpu.VMEM((enc, hid), f32),
            pltpu.VMEM((hid, enc), f32),
            pltpu.VMEM((hid, hid), f32),
            pltpu.VMEM((out, hid), f32),
            *(pltpu.VMEM((r // 2, n), f32) for r, n in sizes),
            *(pltpu.VMEM((n_tile // 2, r // 2, n), f32) for r, n in sizes),
            pltpu.SemaphoreType.DMA((chunks + 10,)),
            pltpu.SemaphoreType.DMA((n_slab,)),
            pltpu.SemaphoreType.DMA((n_slab,)),
            pltpu.SemaphoreType.DMA((3,)),
            pltpu.SemaphoreType.DMA((3,)),
            pltpu.SemaphoreType.DMA((3, n_tile // 2)),
            pltpu.SemaphoreType.DMA((3, n_tile // 2)),
            pltpu.SemaphoreType.DMA((3,)),
            pltpu.SemaphoreType.DMA((3,)),
        ]
        shapes = (
            jax.ShapeDtypeStruct((1, rays_dev), f32),
            jax.ShapeDtypeStruct((enc, hid), f32),
            jax.ShapeDtypeStruct((hid, hid), f32),
            jax.ShapeDtypeStruct((out, hid), f32),
        )
        results = pl.pallas_call(
            functools.partial(kernel, chunks, n_slab, n_tile),
            out_shape=shapes,
            in_specs=[any_space] * 11,
            out_specs=(vmem,) * 4,
            scratch_shapes=scratch,
            compiler_params=pltpu.CompilerParams(
                collective_id=0, has_side_effects=True, vmem_limit_bytes=56 * 2**20
            ),
        )(
            encoded,
            spacing,
            counts,
            row(seg_first),
            row(seg_last),
            row(direction),
            field_in,
            field_mid,
            field_out.transpose(0, 2, 1),
            color_head.T,
            target.T,
        )
        front, g1, g2, g3t = pl.pallas_call(
            hand_on,
            out_shape=shapes,
            in_specs=[vmem] * 4,
            out_specs=(vmem,) * 4,
        )(*results)
        return front, g1[None], g2[None], g3t.T[None]

    return jax.shard_map(
        body,
        mesh=mesh,
        in_specs=(
            P("slab", None, "tile", None),
            P("slab", None, "tile"),
            P("slab", "tile"),
            P("tile"),
            P("tile"),
            P("tile"),
            P("slab", None, None),
            P("slab", None, None),
            P("slab", None, None),
            P(),
            P("tile", None),
        ),
        out_specs=(
            P("slab", "tile"),
            P("slab", None, None),
            P("slab", None, None),
            P("slab", None, None),
        ),
        check_vma=False,
    )
```

```python
import functools

import jax
import jax.numpy as jnp
from jax import lax
from jax.experimental import pallas as pl
from jax.experimental.pallas import tpu as pltpu
from jax.sharding import PartitionSpec as P

MESH = pl.DeviceIdType.MESH
NN = ((1,), (0,))
NT = ((1,), (1,))
LANES = 128


def mm(a, b, dims):
    return lax.dot_general(a, b, (dims, ((), ())), preferred_element_type=jnp.float32)


def running_sum(values):
    rows = values.shape[0]
    row_ids = lax.broadcasted_iota(jnp.int32, values.shape, 0)
    shift = 1
    while shift < rows:
        moved = pltpu.roll(values, shift, axis=0)
        values = values + jnp.where(row_ids >= shift, moved, 0.0)
        shift *= 2
    return values


def kernel(
    chunks,
    n_slab,
    n_tile,
    x_hbm,
    space_hbm,
    counts_hbm,
    first_hbm,
    last_hbm,
    dir_hbm,
    w1_hbm,
    w2_hbm,
    w3t_hbm,
    head_hbm,
    target_hbm,
    front_out,
    g1_out,
    g2_out,
    g3_out,
    x_s,
    space_s,
    ints_s,
    w1_s,
    w2_s,
    w3t_s,
    head_s,
    target_s,
    w1t_s,
    w2t_s,
    head8_s,
    headt_s,
    w3p_s,
    fold_s,
    foldt_s,
    h1_s,
    h2_s,
    b2_s,
    coef_s,
    proj_s,
    stack_s,
    saved_s,
    held_s,
    send_s,
    gather_s,
    g1_s,
    g1t_s,
    g2_s,
    g3_s,
    pair1_s,
    pair2_s,
    pair3_s,
    half1_s,
    half2_s,
    half3_s,
    mid1_s,
    mid2_s,
    mid3_s,
    near1_s,
    near2_s,
    near3_s,
    far1_s,
    far2_s,
    far3_s,
    in_sem,
    ex_send,
    ex_recv,
    pair_send,
    pair_recv,
    swap_send,
    swap_recv,
    pass_send,
    pass_recv,
):
    samples, rays_dev = space_s.shape
    rays = rays_dev // chunks
    cols = samples * rays
    groups = rays // LANES
    me = lax.axis_index("slab")
    tile = lax.axis_index("tile")
    core, ypos = tile % 2, tile // 2
    n_y = n_tile // 2

    barrier = pltpu.get_barrier_semaphore()
    for step in range(1, n_slab):
        pl.semaphore_signal(
            barrier, inc=1, device_id={"slab": (me + step) % n_slab}, device_id_type=MESH
        )
    across = (ypos + 1 - 2 * (ypos % 2), n_y - 1 - ypos)
    mates = [ypos * 2 + 1 - core] + [y * 2 + core for y in across]
    for mate in mates:
        pl.semaphore_signal(barrier, inc=1, device_id={"tile": mate}, device_id_type=MESH)

    small = [
        (w1_hbm.at[0], w1_s),
        (w2_hbm.at[0], w2_s),
        (w3t_hbm.at[0], w3t_s),
        (head_hbm, head_s),
        (space_hbm.at[0], space_s),
        (counts_hbm, ints_s.at[0]),
        (first_hbm, ints_s.at[1]),
        (last_hbm, ints_s.at[2]),
        (dir_hbm, ints_s.at[3]),
        (target_hbm, target_s),
    ]
    loads = [
        pltpu.make_async_copy(src, dst, in_sem.at[chunks + i]) for i, (src, dst) in enumerate(small)
    ]
    x_loads = [
        pltpu.make_async_copy(
            x_hbm.at[0, :, pl.ds(c * rays, rays), :], x_s.at[c], in_sem.at[c]
        )
        for c in range(chunks)
    ]
    loads[0].start()
    x_loads[0].start()
    for load in loads[1:]:
        load.start()
    for load in x_loads[1:]:
        load.start()

    loads[0].wait()
    w1t_s[...] = w1_s[...].T
    loads[1].wait()
    w2t_s[...] = w2_s[...].T
    loads[2].wait()
    loads[3].wait()
    head8_s[...] = jnp.zeros_like(head8_s)
    lane = lax.broadcasted_iota(jnp.int32, (1, LANES), 1)
    head8_s[0:1, :] = (lane == 0).astype(jnp.float32)
    head8_s[1:4, 0 : head_s.shape[1]] = head_s[...]
    headt_s[...] = head8_s[...].T
    width = w3t_s.shape[0]
    folded = lax.dot_general(
        head8_s[:, 0:width],
        w3t_s[...].astype(jnp.float32),
        (NN, ((), ())),
        precision=lax.Precision.HIGHEST,
        preferred_element_type=jnp.float32,
    )
    hi = folded.astype(jnp.bfloat16).astype(jnp.float32)
    mid = (folded - hi).astype(jnp.bfloat16).astype(jnp.float32)
    low = folded - hi - mid
    zeros = jnp.zeros_like(folded)
    w3p_s[...] = jnp.concatenate([hi, mid, low, zeros], axis=0).astype(jnp.bfloat16)
    fold_s[...] = jnp.zeros_like(fold_s)
    fold_s[0:4, :] = hi[0:4]
    fold_s[4:8, :] = hi[0:4]
    fold_s[8:12, :] = mid[0:4]
    foldt_s[...] = fold_s[...].T[:, 0:16].astype(jnp.bfloat16)
    stack_s[...] = jnp.zeros_like(stack_s)
    for load in loads[4:]:
        load.wait()

    row_ids = lax.broadcasted_iota(jnp.int32, (samples, rays), 0)
    tile_rows = lax.broadcasted_iota(jnp.int32, (8, LANES), 0)
    is_trans = (tile_rows % 4) == 0
    identity = is_trans.astype(jnp.float32)

    def spread(v):
        return jnp.where(tile_rows < 4, v[0:1, :], v[4:5, :])

    def ray_slice(c):
        return pl.ds(c * rays, rays)

    def exchange(step, source):
        return pltpu.make_async_remote_copy(
            src_ref=send_s,
            dst_ref=gather_s.at[source],
            send_sem=ex_send.at[step],
            recv_sem=ex_recv.at[source],
            device_id={"slab": (me + step) % n_slab},
            device_id_type=MESH,
        )

    def lanes_of(values, g):
        return values[:, g * LANES : (g + 1) * LANES]

    def later_sum(values, reverse):
        running = running_sum(values)
        return jnp.where(reverse, running - values, running[samples - 1 : samples, :] - running)

    def forward(c):
        x_loads[c].wait()
        x = x_s[c].reshape(cols, x_s.shape[3])
        base = c * cols
        h1 = jnp.maximum(mm(w1t_s[...], x, NT).astype(jnp.bfloat16), 0)
        h1_s[:, pl.ds(base, cols)] = h1
        h2 = jnp.maximum(mm(w2t_s[...], h1, NN).astype(jnp.bfloat16), 0)
        h2_s[:, pl.ds(base, cols)] = h2
        p = mm(w3p_s[...], h2, NN)
        p = p[0:8, :] + (p[8:16, :] + p[16:24, :])
        for j in range(samples):
            for g in range(groups):
                at = j * rays + g * LANES
                proj_s[c, g, 8 * j : 8 * j + 8, :] = p[:, at : at + LANES]
        o0, *ps = (
            jnp.concatenate(
                [proj_s[c, g, pl.ds(k, samples, stride=8), :] for g in range(groups)], 1
            )
            for k in range(4)
        )
        rs = ray_slice(c)
        counts = ints_s[0, :, rs]
        first = ints_s[1, :, rs]
        last = ints_s[2, :, rs]
        reverse = ints_s[3, :, rs] > 0
        active = (first <= me) & (me < last)
        live = ((row_ids < counts) & active).astype(jnp.float32)
        span = space_s[:, rs] * live
        soft = jnp.maximum(o0, 0.0) + jnp.log1p(jnp.exp(-jnp.abs(o0)))
        optical = soft * span
        running = running_sum(optical)
        column = running[samples - 1 : samples, :]
        before = jnp.where(reverse, column - running, running - optical)
        gone = jnp.exp(-before)
        stay = jnp.exp(-optical)
        weights = gone * (1.0 - stay)
        trans = jnp.exp(-column)
        shown = [weights * ps[k] for k in range(3)]
        rows = [trans] + [jnp.sum(shown[k], axis=0, keepdims=True) for k in range(3)]
        for g in range(groups):
            for k in range(4):
                send_s[c, 4 * g + k : 4 * g + k + 1, :] = lanes_of(rows[k], g)
        slope = span * (1.0 / (1.0 + jnp.exp(-o0)))
        spent = gone * stay
        saved_s[c, 0] = weights
        for k in range(3):
            saved_s[c, 1 + k] = slope * (spent * ps[k] - later_sum(shown[k], reverse))
        saved_s[c, 4] = -(trans * slope)

    def hold(c):
        base = c * cols
        block = 32
        for f in range(0, h2_s.shape[0], block):
            sums = [None] * 5
            for j in range(samples):
                h2 = h2_s[f : f + block, pl.ds(base + j * rays, rays)].astype(jnp.float32)
                for m in range(5):
                    term = h2 * saved_s[c, m, j : j + 1, :]
                    sums[m] = term if j == 0 else sums[m] + term
            for m in range(5):
                held_s[c, m, f : f + block, :] = sums[m]

    def compose(c):
        rs = ray_slice(c)
        rev = jnp.where(
            tile_rows < 4,
            jnp.broadcast_to(ints_s[3, :, pl.ds(c * rays, LANES)], (8, LANES)),
            jnp.broadcast_to(ints_s[3, :, pl.ds(c * rays + (groups - 1) * LANES, LANES)], (8, LANES)),
        ) > 0

        def step_of(run, item, item_first):
            run_t, item_t = spread(run), spread(item)
            run_first = jnp.where(is_trans, 0.0, run) + run_t * item
            late_first = jnp.where(is_trans, 0.0, item) + item_t * run
            return jnp.where(item_first, late_first, run_first)

        low = high = identity
        for s in range(n_slab):
            t = n_slab - 1 - s
            low = step_of(low, jnp.where(s < me, gather_s[s, c], identity), rev)
            high = step_of(high, jnp.where(t > me, gather_s[t, c], identity), jnp.logical_not(rev))
        own = send_s[c]
        front = jnp.where(rev, high, low)
        back = jnp.where(rev, low, high)
        front_t, own_t = spread(front), spread(own)
        logits = front + front_t * own + (front_t * own_t) * back
        shade = 1.0 / (1.0 + jnp.exp(-logits))
        target = jnp.zeros((8, LANES), jnp.float32)
        for g in range(groups):
            for k in range(3):
                target = jnp.where(
                    tile_rows == 4 * g + 1 + k,
                    target_s[k : k + 1, pl.ds(c * rays + g * LANES, LANES)],
                    target,
                )
        grad3 = jnp.where(is_trans, 0.0, (shade - target) * (1.0 / rays_dev) * shade * (1.0 - shade))
        seg = front_t * grad3
        dots = seg * back
        fronts, grads, seg_t = [], [[], [], []], []
        for g in range(groups):
            r = 4 * g
            fronts.append(front[r : r + 1, :])
            for k in range(3):
                grads[k].append(seg[r + 1 + k : r + 2 + k, :])
            seg_t.append(dots[r + 1 : r + 2, :] + dots[r + 2 : r + 3, :] + dots[r + 3 : r + 4, :])
        join = lambda parts: jnp.concatenate(parts, 1)
        front_out[:, rs] = join(fronts)
        return [join(grads[k]) for k in range(3)] + [join(seg_t)]

    def coefficients(c, cot):
        weights = saved_s[c, 0]
        density = (
            cot[0] * saved_s[c, 1] + cot[1] * saved_s[c, 2] + cot[2] * saved_s[c, 3] + cot[3] * saved_s[c, 4]
        )
        for m, value in enumerate([density] + [cot[k] * weights for k in range(3)]):
            hi = value.astype(jnp.bfloat16).astype(jnp.float32)
            for g in range(groups):
                for row, part in ((m, hi), (4 + m, value - hi), (8 + m, hi)):
                    stack_s[c, g, row * samples : (row + 1) * samples, :] = lanes_of(part, g)
        for j in range(samples):
            for g in range(groups):
                coef_s[:, pl.ds(c * cols + j * rays + g * LANES, LANES)] = jnp.concatenate(
                    [
                        stack_s[c, g, pl.ds(j, 8, stride=samples), :],
                        stack_s[c, g, pl.ds(8 * samples + j, 8, stride=samples), :],
                    ],
                    0,
                ).astype(jnp.bfloat16)

    def grad_out(cots):
        hid = h2_s.shape[0]
        block = 32
        column = lax.broadcasted_iota(jnp.int32, (block, LANES), 1)
        for f in range(0, hid, block):
            parts = [0.0] * 4
            for c in range(chunks):
                for g in range(groups):
                    at = pl.ds(g * LANES, LANES)
                    shown = held_s[c, 0, f : f + block, at]
                    for k in range(3):
                        parts[k] = parts[k] + shown * lanes_of(cots[c][k], g)
                    for m in range(4):
                        parts[3] = parts[3] + held_s[c, 1 + m, f : f + block, at] * lanes_of(cots[c][m], g)
            packed = jnp.zeros((block, LANES), jnp.float32)
            for k in range(4):
                packed = jnp.where(column == k, jnp.sum(parts[k], axis=1, keepdims=True), packed)
            held_s[0, 0, f : f + block, 0:LANES] = packed
        sums = held_s[0, 0, :, 0:LANES].T
        first_row = lax.broadcasted_iota(jnp.int32, (width, 1), 0) == 0
        total = jnp.where(first_row, sums[3:4, :], 0.0)
        for k in range(3):
            total = total + headt_s[0:width, 1 + k : 2 + k] * sums[k : k + 1, :]
        g3_s[...] = total

    def backward_two(c):
        base = c * cols
        b2 = mm(foldt_s[...], coef_s[:, pl.ds(base, cols)], NN).astype(jnp.bfloat16)
        b2 = jnp.where(h2_s[:, pl.ds(base, cols)] > 0, b2, 0)
        b2_s[:, pl.ds(base, cols)] = b2
        part = mm(h1_s[:, pl.ds(base, cols)], b2, NT)
        g2_s[...] = part if c == 0 else g2_s[...] + part

    def backward_one(c):
        base = c * cols
        b1 = mm(w2_s[...], b2_s[:, pl.ds(base, cols)], NN).astype(jnp.bfloat16)
        b1 = jnp.where(h1_s[:, pl.ds(base, cols)] > 0, b1, 0)
        part = mm(b1, x_s[c].reshape(cols, x_s.shape[3]), NN)
        g1t_s[...] = part if c == 0 else g1t_s[...] + part

    grads = (
        (g1_s, pair1_s, half1_s, near1_s, mid1_s, far1_s, g1_out),
        (g2_s, pair2_s, half2_s, near2_s, mid2_s, far2_s, g2_out),
        (g3_s, pair3_s, half3_s, near3_s, mid3_s, far3_s, g3_out),
    )
    partner = ypos * 2 + 1 - core

    def half_rows(i, k):
        rows = grads[i][1].shape[0]
        return pl.ds(pl.multiple_of(k * rows, 8), rows)

    def pair_copy(i):
        whole, pair = grads[i][:2]
        return pltpu.make_async_remote_copy(
            src_ref=whole.at[half_rows(i, 1 - core), :],
            dst_ref=pair,
            send_sem=pair_send.at[i],
            recv_sem=pair_recv.at[i],
            device_id={"tile": partner},
            device_id_type=MESH,
        )

    def swap_copy(i, stage, part):
        source, target = (grads[i][2:4], grads[i][4:6])[stage]
        rows = source.shape[0] // 2
        at = pl.ds(part * rows, rows)
        return pltpu.make_async_remote_copy(
            src_ref=source.at[at, :],
            dst_ref=target.at[at, :],
            send_sem=swap_send.at[i, stage, part],
            recv_sem=swap_recv.at[i, stage, part],
            device_id={"tile": across[(stage + part) % 2] * 2 + core},
            device_id_type=MESH,
        )

    def pass_copy(i, k):
        out = grads[i][6]
        at = half_rows(i, k)
        return pltpu.make_async_remote_copy(
            src_ref=out.at[at, :],
            dst_ref=out.at[at, :],
            send_sem=pass_send.at[i],
            recv_sem=pass_recv.at[i],
            device_id={"tile": partner},
            device_id_type=MESH,
        )

    def swap_first(i):
        whole, pair, half = grads[i][:3]
        pair_copy(i).wait_recv()
        half[...] = whole[half_rows(i, core), :] + pair[...]
        for part in range(2):
            swap_copy(i, 0, part).start()

    def swap_second(i):
        half, near, mid = grads[i][2:5]
        rows = half.shape[0] // 2
        for part in range(2):
            swap_copy(i, 0, part).wait_recv()
            at = slice(part * rows, (part + 1) * rows)
            mid[at, :] = half[at, :] + near[at, :]
            swap_copy(i, 1, part).start()

    def finish_half(i):
        mid, far, out = grads[i][4:]
        for part in range(2):
            swap_copy(i, 1, part).wait_recv()
        out[half_rows(i, core), :] = mid[...] + far[...]
        pass_copy(i, core).start()

    for c in range(chunks):
        forward(c)
    pl.semaphore_wait(barrier, n_slab - 1 + len(mates))
    for step in range(1, n_slab):
        exchange(step, me).start()
    gather_s[me] = send_s[...]
    for c in range(chunks):
        hold(c)
    for step in range(1, n_slab):
        exchange(step, (me + n_slab - step) % n_slab).wait_recv()
    cots = [compose(c) for c in range(chunks)]
    for c in range(chunks):
        coefficients(c, cots[c])
    grad_out(cots)
    pair_copy(2).start()
    backward_two(0)
    swap_first(2)
    for c in range(1, chunks):
        backward_two(c)
    pair_copy(1).start()
    backward_one(0)
    swap_first(1)
    for c in range(1, chunks):
        backward_one(c)
    g1_s[...] = g1t_s[...].T
    pair_copy(0).start()
    swap_second(2)
    swap_first(0)
    swap_second(1)
    finish_half(2)
    swap_second(0)
    finish_half(1)
    finish_half(0)
    for i in (2, 1, 0):
        pass_copy(i, 1 - core).wait_recv()
    for i in (2, 1, 0):
        pass_copy(i, core).wait_send()
        pair_copy(i).wait_send()
        for stage in range(2):
            for part in range(2):
                swap_copy(i, stage, part).wait_send()
    for step in range(1, n_slab):
        exchange(step, me).wait_send()


def hand_on(*refs):
    half = len(refs) // 2
    for src, dst in zip(refs[:half], refs[half:]):
        dst[...] = src[...]


def solution(mesh):
    n_slab, n_tile = mesh.shape["slab"], mesh.shape["tile"]
    chunks = 2

    def body(
        encoded,
        spacing,
        counts,
        seg_first,
        seg_last,
        direction,
        field_in,
        field_mid,
        field_out,
        color_head,
        target,
    ):
        _, samples, rays_dev, enc = encoded.shape
        hid, out = field_out.shape[1:]
        rays = rays_dev // chunks
        total = samples * rays_dev
        f32, bf16 = jnp.float32, jnp.bfloat16
        row = lambda v: v.reshape(1, rays_dev)
        sizes = ((enc, hid), (hid, hid), (out, hid))
        any_space = pl.BlockSpec(memory_space=pl.ANY)
        vmem = pl.BlockSpec(memory_space=pltpu.VMEM)
        scratch = [
            pltpu.VMEM((chunks, samples, rays, enc), bf16),
            pltpu.VMEM((samples, rays_dev), f32),
            pltpu.VMEM((4, 1, rays_dev), jnp.int32),
            pltpu.VMEM((enc, hid), bf16),
            pltpu.VMEM((hid, hid), bf16),
            pltpu.VMEM((out, hid), bf16),
            pltpu.VMEM((3, out), f32),
            pltpu.VMEM((3, rays_dev), f32),
            pltpu.VMEM((hid, enc), bf16),
            pltpu.VMEM((hid, hid), bf16),
            pltpu.VMEM((8, LANES), f32),
            pltpu.VMEM((LANES, 8), f32),
            pltpu.VMEM((32, hid), bf16),
            pltpu.VMEM((LANES, hid), f32),
            pltpu.VMEM((hid, 16), bf16),
            pltpu.VMEM((hid, total), bf16),
            pltpu.VMEM((hid, total), bf16),
            pltpu.VMEM((hid, total), bf16),
            pltpu.VMEM((16, total), bf16),
            pltpu.VMEM((chunks, rays // LANES, 8 * samples, LANES), f32),
            pltpu.VMEM((chunks, rays // LANES, 16 * samples, LANES), f32),
            pltpu.VMEM((chunks, 5, samples, rays), f32),
            pltpu.VMEM((chunks, 5, hid, rays), f32),
            pltpu.VMEM((chunks, 8, LANES), f32),
            pltpu.VMEM((n_slab, chunks, 8, LANES), f32),
            pltpu.VMEM((enc, hid), f32),
            pltpu.VMEM((hid, enc), f32),
            pltpu.VMEM((hid, hid), f32),
            pltpu.VMEM((out, hid), f32),
            *(pltpu.VMEM((r // 2, n), f32) for r, n in sizes),
            *(pltpu.VMEM((r // 2, n), f32) for r, n in sizes),
            *(pltpu.VMEM((r // 2, n), f32) for r, n in sizes),
            *(pltpu.VMEM((r // 2, n), f32) for r, n in sizes),
            *(pltpu.VMEM((r // 2, n), f32) for r, n in sizes),
            pltpu.SemaphoreType.DMA((chunks + 10,)),
            pltpu.SemaphoreType.DMA((n_slab,)),
            pltpu.SemaphoreType.DMA((n_slab,)),
            pltpu.SemaphoreType.DMA((3,)),
            pltpu.SemaphoreType.DMA((3,)),
            pltpu.SemaphoreType.DMA((3, 2, 2)),
            pltpu.SemaphoreType.DMA((3, 2, 2)),
            pltpu.SemaphoreType.DMA((3,)),
            pltpu.SemaphoreType.DMA((3,)),
        ]
        shapes = (
            jax.ShapeDtypeStruct((1, rays_dev), f32),
            jax.ShapeDtypeStruct((enc, hid), f32),
            jax.ShapeDtypeStruct((hid, hid), f32),
            jax.ShapeDtypeStruct((out, hid), f32),
        )
        results = pl.pallas_call(
            functools.partial(kernel, chunks, n_slab, n_tile),
            out_shape=tuple(pltpu.VMEM(q.shape, q.dtype) for q in shapes),
            in_specs=[any_space] * 11,
            out_specs=(vmem,) * 4,
            scratch_shapes=scratch,
            compiler_params=pltpu.CompilerParams(
                collective_id=0, has_side_effects=True, vmem_limit_bytes=56 * 2**20
            ),
        )(
            encoded,
            spacing,
            counts,
            row(seg_first),
            row(seg_last),
            row(direction),
            field_in,
            field_mid,
            field_out.transpose(0, 2, 1),
            color_head.T,
            target.T,
        )
        front, g1, g2, g3t = pl.pallas_call(
            hand_on,
            out_shape=shapes,
            in_specs=[vmem] * 4,
            out_specs=(vmem,) * 4,
        )(*(pltpu.with_memory_space_constraint(r, pltpu.VMEM) for r in results))
        return front, g1[None], g2[None], g3t.T[None]

    return jax.shard_map(
        body,
        mesh=mesh,
        in_specs=(
            P("slab", None, "tile", None),
            P("slab", None, "tile"),
            P("slab", "tile"),
            P("tile"),
            P("tile"),
            P("tile"),
            P("slab", None, None),
            P("slab", None, None),
            P("slab", None, None),
            P(),
            P("tile", None),
        ),
        out_specs=(
            P("slab", "tile"),
            P("slab", None, None),
            P("slab", None, None),
            P("slab", None, None),
        ),
        check_vma=False,
    )
```

```python
import functools
import math

import jax
import jax.numpy as jnp
from jax import lax
from jax.experimental import pallas as pl
from jax.experimental.pallas import tpu as pltpu
from jax.sharding import PartitionSpec as P

MESH = pl.DeviceIdType.MESH
NN = ((1,), (0,))
NT = ((1,), (1,))
LANES = 128


def mm(a, b, dims):
    return lax.dot_general(a, b, (dims, ((), ())), preferred_element_type=jnp.float32)


def running_sum(values):
    rows = values.shape[0]
    row_ids = lax.broadcasted_iota(jnp.int32, values.shape, 0)
    shift = 1
    while shift < rows:
        moved = pltpu.roll(values, shift, axis=0)
        values = values + jnp.where(row_ids >= shift, moved, 0.0)
        shift *= 2
    return values


def kernel(
    chunks,
    n_slab,
    n_tile,
    x_hbm,
    space_hbm,
    counts_hbm,
    first_hbm,
    last_hbm,
    dir_hbm,
    w1_hbm,
    w2_hbm,
    w3t_hbm,
    head_hbm,
    target_hbm,
    front_out,
    g1_out,
    g2_out,
    g3_out,
    x_s,
    space_s,
    ints_s,
    w1_s,
    w2_s,
    w3t_s,
    head_s,
    target_s,
    w1t_s,
    w2t_s,
    head8_s,
    headt_s,
    w3p_s,
    fold_s,
    foldt_s,
    h1_s,
    h2_s,
    b2_s,
    coef_s,
    proj_s,
    stack_s,
    saved_s,
    held_s,
    send_s,
    gather_s,
    g1_s,
    g1t_s,
    g2_s,
    g3_s,
    pair1_s,
    pair2_s,
    pair3_s,
    mid1_s,
    mid2_s,
    mid3_s,
    near1_s,
    near2_s,
    near3_s,
    far1_s,
    far2_s,
    far3_s,
    other1_s,
    other3_s,
    half2_s,
    in_sem,
    ex_send,
    ex_recv,
    pair_send,
    pair_recv,
    swap_send,
    swap_recv,
    pass_send,
    pass_recv,
):
    samples, rays_dev = space_s.shape
    rays = rays_dev // chunks
    cols = samples * rays
    groups = rays // LANES
    me = lax.axis_index("slab")
    tile = lax.axis_index("tile")
    core, ypos = tile % 2, tile // 2
    n_y = n_tile // 2

    barrier = pltpu.get_barrier_semaphore()
    for step in range(1, n_slab):
        pl.semaphore_signal(
            barrier, inc=1, device_id={"slab": (me + step) % n_slab}, device_id_type=MESH
        )
    across = (ypos + 1 - 2 * (ypos % 2), n_y - 1 - ypos)
    mates = [ypos * 2 + 1 - core] + [y * 2 + c for y in across for c in (core, 1 - core)]
    for mate in mates:
        pl.semaphore_signal(barrier, inc=1, device_id={"tile": mate}, device_id_type=MESH)

    small = [
        (w1_hbm.at[0], w1_s),
        (w2_hbm.at[0], w2_s),
        (w3t_hbm.at[0], w3t_s),
        (head_hbm, head_s),
        (space_hbm.at[0], space_s),
        (counts_hbm, ints_s.at[0]),
        (first_hbm, ints_s.at[1]),
        (last_hbm, ints_s.at[2]),
        (dir_hbm, ints_s.at[3]),
        (target_hbm, target_s),
    ]
    loads = [
        pltpu.make_async_copy(src, dst, in_sem.at[chunks + i]) for i, (src, dst) in enumerate(small)
    ]
    x_loads = [
        pltpu.make_async_copy(
            x_hbm.at[0, :, pl.ds(c * rays, rays), :], x_s.at[c], in_sem.at[c]
        )
        for c in range(chunks)
    ]
    loads[0].start()
    x_loads[0].start()
    for load in loads[1:]:
        load.start()
    for load in x_loads[1:]:
        load.start()

    loads[0].wait()
    w1t_s[...] = w1_s[...].T
    loads[1].wait()
    w2t_s[...] = w2_s[...].T
    loads[2].wait()
    loads[3].wait()
    head8_s[...] = jnp.zeros_like(head8_s)
    lane = lax.broadcasted_iota(jnp.int32, (1, LANES), 1)
    head8_s[0:1, :] = (lane == 0).astype(jnp.float32)
    head8_s[1:4, 0 : head_s.shape[1]] = head_s[...]
    headt_s[...] = head8_s[...].T
    width = w3t_s.shape[0]
    folded = lax.dot_general(
        head8_s[:, 0:width],
        w3t_s[...].astype(jnp.float32),
        (NN, ((), ())),
        precision=lax.Precision.HIGHEST,
        preferred_element_type=jnp.float32,
    )
    hi = folded.astype(jnp.bfloat16).astype(jnp.float32)
    mid = (folded - hi).astype(jnp.bfloat16).astype(jnp.float32)
    low = folded - hi - mid
    zeros = jnp.zeros_like(folded)
    w3p_s[...] = jnp.concatenate([hi, mid, low, zeros], axis=0).astype(jnp.bfloat16)
    fold_s[...] = jnp.zeros_like(fold_s)
    fold_s[0:4, :] = hi[0:4]
    fold_s[4:8, :] = hi[0:4]
    fold_s[8:12, :] = mid[0:4]
    foldt_s[...] = fold_s[...].T[:, 0:16].astype(jnp.bfloat16)
    stack_s[...] = jnp.zeros_like(stack_s)
    for load in loads[4:]:
        load.wait()

    row_ids = lax.broadcasted_iota(jnp.int32, (samples, rays), 0)
    tile_rows = lax.broadcasted_iota(jnp.int32, (8, LANES), 0)
    is_trans = (tile_rows % 4) == 0
    identity = is_trans.astype(jnp.float32)

    def spread(v):
        return jnp.where(tile_rows < 4, v[0:1, :], v[4:5, :])

    def ray_slice(c):
        return pl.ds(c * rays, rays)

    side = math.isqrt(n_slab)
    near = lambda d: min(d, side - d)
    moves = sorted(
        ((dx, dz) for dx in range(side) for dz in range(side) if dx or dz),
        key=lambda d: -near(d[0]) - near(d[1]),
    )

    def slab_at(dx, dz):
        return (me // side + dx) % side * side + (me % side + dz) % side

    def exchange(step, source):
        return pltpu.make_async_remote_copy(
            src_ref=send_s,
            dst_ref=gather_s.at[source],
            send_sem=ex_send.at[step],
            recv_sem=ex_recv.at[source],
            device_id={"slab": slab_at(*moves[step])},
            device_id_type=MESH,
        )

    def origin(step):
        dx, dz = moves[step]
        return slab_at(side - dx, side - dz)

    def lanes_of(values, g):
        return values[:, g * LANES : (g + 1) * LANES]

    def later_sum(values, reverse):
        running = running_sum(values)
        return jnp.where(reverse, running - values, running[samples - 1 : samples, :] - running)

    def forward_samples(c):
        x_loads[c].wait()
        x = x_s[c].reshape(cols, x_s.shape[3])
        base = c * cols
        h1 = jnp.maximum(mm(w1t_s[...], x, NT).astype(jnp.bfloat16), 0)
        h1_s[:, pl.ds(base, cols)] = h1
        h2 = jnp.maximum(mm(w2t_s[...], h1, NN).astype(jnp.bfloat16), 0)
        h2_s[:, pl.ds(base, cols)] = h2
        p = mm(w3p_s[...], h2, NN)
        p = p[0:8, :] + (p[8:16, :] + p[16:24, :])
        for j in range(samples):
            for g in range(groups):
                at = j * rays + g * LANES
                proj_s[c, g, 8 * j : 8 * j + 8, :] = p[:, at : at + LANES]

    def forward_rays(c):
        o0, *ps = (
            jnp.concatenate(
                [proj_s[c, g, pl.ds(k, samples, stride=8), :] for g in range(groups)], 1
            )
            for k in range(4)
        )
        rs = ray_slice(c)
        counts = ints_s[0, :, rs]
        first = ints_s[1, :, rs]
        last = ints_s[2, :, rs]
        reverse = ints_s[3, :, rs] > 0
        active = (first <= me) & (me < last)
        live = ((row_ids < counts) & active).astype(jnp.float32)
        span = space_s[:, rs] * live
        soft = jnp.maximum(o0, 0.0) + jnp.log1p(jnp.exp(-jnp.abs(o0)))
        optical = soft * span
        running = running_sum(optical)
        column = running[samples - 1 : samples, :]
        before = jnp.where(reverse, column - running, running - optical)
        gone = jnp.exp(-before)
        stay = jnp.exp(-optical)
        weights = gone * (1.0 - stay)
        trans = jnp.exp(-column)
        shown = [weights * ps[k] for k in range(3)]
        rows = [trans] + [jnp.sum(shown[k], axis=0, keepdims=True) for k in range(3)]
        for g in range(groups):
            for k in range(4):
                send_s[c, 4 * g + k : 4 * g + k + 1, :] = lanes_of(rows[k], g)
        return o0, ps, span, gone * stay, weights, shown, trans, reverse

    def slopes(c, values):
        o0, ps, span, spent, weights, shown, trans, reverse = values
        slope = span * (1.0 / (1.0 + jnp.exp(-o0)))
        saved_s[c, 0] = weights
        for k in range(3):
            saved_s[c, 1 + k] = slope * (spent * ps[k] - later_sum(shown[k], reverse))
        saved_s[c, 4] = -(trans * slope)

    def hold(c):
        base = c * cols
        block = 32
        for f in range(0, h2_s.shape[0], block):
            sums = [None] * 5
            for j in range(samples):
                h2 = h2_s[f : f + block, pl.ds(base + j * rays, rays)].astype(jnp.float32)
                for m in range(5):
                    term = h2 * saved_s[c, m, j : j + 1, :]
                    sums[m] = term if j == 0 else sums[m] + term
            for m in range(5):
                held_s[c, m, f : f + block, :] = sums[m]

    def compose(c):
        rs = ray_slice(c)
        rev = jnp.where(
            tile_rows < 4,
            jnp.broadcast_to(ints_s[3, :, pl.ds(c * rays, LANES)], (8, LANES)),
            jnp.broadcast_to(ints_s[3, :, pl.ds(c * rays + (groups - 1) * LANES, LANES)], (8, LANES)),
        ) > 0

        def step_of(run, item, item_first):
            run_t, item_t = spread(run), spread(item)
            run_first = jnp.where(is_trans, 0.0, run) + run_t * item
            late_first = jnp.where(is_trans, 0.0, item) + item_t * run
            return jnp.where(item_first, late_first, run_first)

        low = high = identity
        for s in range(n_slab):
            t = n_slab - 1 - s
            low = step_of(low, jnp.where(s < me, gather_s[s, c], identity), rev)
            high = step_of(high, jnp.where(t > me, gather_s[t, c], identity), jnp.logical_not(rev))
        own = send_s[c]
        front = jnp.where(rev, high, low)
        back = jnp.where(rev, low, high)
        front_t, own_t = spread(front), spread(own)
        logits = front + front_t * own + (front_t * own_t) * back
        shade = 1.0 / (1.0 + jnp.exp(-logits))
        target = jnp.zeros((8, LANES), jnp.float32)
        for g in range(groups):
            for k in range(3):
                target = jnp.where(
                    tile_rows == 4 * g + 1 + k,
                    target_s[k : k + 1, pl.ds(c * rays + g * LANES, LANES)],
                    target,
                )
        grad3 = jnp.where(is_trans, 0.0, (shade - target) * (1.0 / rays_dev) * shade * (1.0 - shade))
        seg = front_t * grad3
        dots = seg * back
        fronts, grads, seg_t = [], [[], [], []], []
        for g in range(groups):
            r = 4 * g
            fronts.append(front[r : r + 1, :])
            for k in range(3):
                grads[k].append(seg[r + 1 + k : r + 2 + k, :])
            seg_t.append(dots[r + 1 : r + 2, :] + dots[r + 2 : r + 3, :] + dots[r + 3 : r + 4, :])
        join = lambda parts: jnp.concatenate(parts, 1)
        front_out[:, rs] = join(fronts)
        return [join(grads[k]) for k in range(3)] + [join(seg_t)]

    def coefficients(c, cot):
        weights = saved_s[c, 0]
        density = (
            cot[0] * saved_s[c, 1] + cot[1] * saved_s[c, 2] + cot[2] * saved_s[c, 3] + cot[3] * saved_s[c, 4]
        )
        for m, value in enumerate([density] + [cot[k] * weights for k in range(3)]):
            hi = value.astype(jnp.bfloat16).astype(jnp.float32)
            for g in range(groups):
                for row, part in ((m, hi), (4 + m, value - hi), (8 + m, hi)):
                    stack_s[c, g, row * samples : (row + 1) * samples, :] = lanes_of(part, g)
        for j in range(samples):
            for g in range(groups):
                coef_s[:, pl.ds(c * cols + j * rays + g * LANES, LANES)] = jnp.concatenate(
                    [
                        stack_s[c, g, pl.ds(j, 8, stride=samples), :],
                        stack_s[c, g, pl.ds(8 * samples + j, 8, stride=samples), :],
                    ],
                    0,
                ).astype(jnp.bfloat16)

    def grad_out(cots):
        hid = h2_s.shape[0]
        block = 32
        column = lax.broadcasted_iota(jnp.int32, (block, LANES), 1)
        for f in range(0, hid, block):
            parts = [0.0] * 4
            for c in range(chunks):
                for g in range(groups):
                    at = pl.ds(g * LANES, LANES)
                    shown = held_s[c, 0, f : f + block, at]
                    for k in range(3):
                        parts[k] = parts[k] + shown * lanes_of(cots[c][k], g)
                    for m in range(4):
                        parts[3] = parts[3] + held_s[c, 1 + m, f : f + block, at] * lanes_of(cots[c][m], g)
            packed = jnp.zeros((block, LANES), jnp.float32)
            for k in range(4):
                packed = jnp.where(column == k, jnp.sum(parts[k], axis=1, keepdims=True), packed)
            held_s[0, 0, f : f + block, 0:LANES] = packed
        sums = held_s[0, 0, :, 0:LANES].T
        first_row = lax.broadcasted_iota(jnp.int32, (width, 1), 0) == 0
        total = jnp.where(first_row, sums[3:4, :], 0.0)
        for k in range(3):
            total = total + headt_s[0:width, 1 + k : 2 + k] * sums[k : k + 1, :]
        g3_s[...] = total

    def backward_two(c):
        base = c * cols
        b2 = mm(foldt_s[...], coef_s[:, pl.ds(base, cols)], NN).astype(jnp.bfloat16)
        b2 = jnp.where(h2_s[:, pl.ds(base, cols)] > 0, b2, 0)
        b2_s[:, pl.ds(base, cols)] = b2
        part = mm(h1_s[:, pl.ds(base, cols)], b2, NT)
        g2_s[...] = part if c == 0 else g2_s[...] + part

    def backward_one(c):
        base = c * cols
        b1 = mm(w2_s[...], b2_s[:, pl.ds(base, cols)], NN).astype(jnp.bfloat16)
        b1 = jnp.where(h1_s[:, pl.ds(base, cols)] > 0, b1, 0)
        part = mm(b1, x_s[c].reshape(cols, x_s.shape[3]), NN)
        g1t_s[...] = part if c == 0 else g1t_s[...] + part

    grads = (
        (g1_s, pair1_s, near1_s, mid1_s, far1_s, other1_s, g1_out),
        (g2_s, pair2_s, near2_s, mid2_s, far2_s, None, g2_out),
        (g3_s, pair3_s, near3_s, mid3_s, far3_s, other3_s, g3_out),
    )
    partner = ypos * 2 + 1 - core

    def half_rows(i, k):
        rows = grads[i][1].shape[0]
        return pl.ds(pl.multiple_of(k * rows, 8), rows)

    def part_rows(i, part):
        rows = grads[i][1].shape[0] // 2
        return pl.ds(part * rows, rows)

    def pair_copy(i):
        whole, pair = grads[i][:2]
        return pltpu.make_async_remote_copy(
            src_ref=whole.at[half_rows(i, 1 - core), :],
            dst_ref=pair,
            send_sem=pair_send.at[i],
            recv_sem=pair_recv.at[i],
            device_id={"tile": partner},
            device_id_type=MESH,
        )

    def swap_copy(i, stage, part, turn):
        whole, pair, near, mid, far = grads[i][:5]
        rows = pair.shape[0] // 2
        if stage == 0 and i == 1:
            source, target = half2_s.at[part_rows(i, part), :], near
        elif stage == 0:
            half = 1 - core if turn else core
            at = pl.multiple_of(half * (2 * rows) + part * rows, 8)
            source, target = whole.at[pl.ds(at, rows), :], near
        else:
            source, target = mid.at[part_rows(i, part), :], far
        return pltpu.make_async_remote_copy(
            src_ref=source,
            dst_ref=target.at[turn, part_rows(i, part), :],
            send_sem=swap_send.at[i, stage, part, turn],
            recv_sem=swap_recv.at[i, stage, part, turn],
            device_id={"tile": across[(stage + part) % 2] * 2 + (1 - core if turn else core)},
            device_id_type=MESH,
        )

    def pass_copy(i):
        source, target = grads[i][3], grads[i][5]
        if i == 1:
            source = target = g2_out.at[half_rows(1, core), :]
        return pltpu.make_async_remote_copy(
            src_ref=source,
            dst_ref=target,
            send_sem=pass_send.at[i],
            recv_sem=pass_recv.at[i],
            device_id={"tile": partner},
            device_id_type=MESH,
        )

    def send_own(i):
        for turn in range(2):
            for part in range(2):
                swap_copy(i, 0, part, turn).start()
        pair_copy(i).start()

    def send_sums(i):
        whole, pair, near, mid = grads[i][:4]
        rows = pair.shape[0] // 2
        pair_copy(i).wait_recv()
        for part in range(2):
            for turn in range(2):
                swap_copy(i, 0, part, turn).wait_recv()
            at = part_rows(i, part)
            own = whole[pl.ds(pl.multiple_of(core * (2 * rows) + part * rows, 8), rows), :]
            mid[at, :] = (own + pair[at, :]) + (near[0, at, :] + near[1, at, :])
            for turn in range(2):
                swap_copy(i, 1, part, turn).start()
        pass_copy(i).start()

    def lean_first():
        pair_copy(1).wait_recv()
        half2_s[...] = g2_s[half_rows(1, core), :] + pair2_s[...]
        for part in range(2):
            swap_copy(1, 0, part, 0).start()

    def lean_second():
        for part in range(2):
            swap_copy(1, 0, part, 0).wait_recv()
            at = part_rows(1, part)
            mid2_s[at, :] = half2_s[at, :] + near2_s[0, at, :]
            swap_copy(1, 1, part, 0).start()

    def lean_third():
        for part in range(2):
            swap_copy(1, 1, part, 0).wait_recv()
        g2_out[half_rows(1, core), :] = mid2_s[...] + far2_s[0]
        pass_copy(1).start()

    def finish(i):
        mid, far, other, out = grads[i][3:]
        for turn in range(2):
            for part in range(2):
                swap_copy(i, 1, part, turn).wait_recv()
        out[half_rows(i, core), :] = mid[...] + far[0]
        pass_copy(i).wait_recv()
        out[half_rows(i, 1 - core), :] = other[...] + far[1]

    for c in range(chunks):
        forward_samples(c)
    values = [forward_rays(c) for c in range(chunks)]
    pl.semaphore_wait(barrier, n_slab - 1 + len(mates))
    for step in range(n_slab - 1):
        exchange(step, me).start()
    gather_s[me] = send_s[...]
    for c in range(chunks):
        slopes(c, values[c])
    for c in range(chunks):
        hold(c)
    for step in range(n_slab - 1):
        exchange(step, origin(step)).wait_recv()
    cots = [compose(c) for c in range(chunks)]
    coefficients(0, cots[0])
    backward_two(0)
    coefficients(1, cots[1])
    grad_out(cots)
    send_own(2)
    backward_two(1)
    pair_copy(1).start()
    backward_one(0)
    lean_first()
    backward_one(1)
    g1_s[...] = g1t_s[...].T
    send_own(0)
    send_sums(2)
    lean_second()
    send_sums(0)
    finish(2)
    lean_third()
    finish(0)
    pass_copy(1).wait_recv()
    for i in (2, 1, 0):
        pass_copy(i).wait_send()
        pair_copy(i).wait_send()
        for stage in range(2):
            for part in range(2):
                for turn in range(1 if i == 1 else 2):
                    swap_copy(i, stage, part, turn).wait_send()
    for step in range(n_slab - 1):
        exchange(step, me).wait_send()


def hand_on(*refs):
    half = len(refs) // 2
    for src, dst in zip(refs[:half], refs[half:]):
        dst[...] = src[...]


def solution(mesh):
    n_slab, n_tile = mesh.shape["slab"], mesh.shape["tile"]
    chunks = 2

    def body(
        encoded,
        spacing,
        counts,
        seg_first,
        seg_last,
        direction,
        field_in,
        field_mid,
        field_out,
        color_head,
        target,
    ):
        _, samples, rays_dev, enc = encoded.shape
        hid, out = field_out.shape[1:]
        rays = rays_dev // chunks
        total = samples * rays_dev
        f32, bf16 = jnp.float32, jnp.bfloat16
        row = lambda v: v.reshape(1, rays_dev)
        sizes = ((enc, hid), (hid, hid), (out, hid))
        any_space = pl.BlockSpec(memory_space=pl.ANY)
        vmem = pl.BlockSpec(memory_space=pltpu.VMEM)
        scratch = [
            pltpu.VMEM((chunks, samples, rays, enc), bf16),
            pltpu.VMEM((samples, rays_dev), f32),
            pltpu.VMEM((4, 1, rays_dev), jnp.int32),
            pltpu.VMEM((enc, hid), bf16),
            pltpu.VMEM((hid, hid), bf16),
            pltpu.VMEM((out, hid), bf16),
            pltpu.VMEM((3, out), f32),
            pltpu.VMEM((3, rays_dev), f32),
            pltpu.VMEM((hid, enc), bf16),
            pltpu.VMEM((hid, hid), bf16),
            pltpu.VMEM((8, LANES), f32),
            pltpu.VMEM((LANES, 8), f32),
            pltpu.VMEM((32, hid), bf16),
            pltpu.VMEM((LANES, hid), f32),
            pltpu.VMEM((hid, 16), bf16),
            pltpu.VMEM((hid, total), bf16),
            pltpu.VMEM((hid, total), bf16),
            pltpu.VMEM((hid, total), bf16),
            pltpu.VMEM((16, total), bf16),
            pltpu.VMEM((chunks, rays // LANES, 8 * samples, LANES), f32),
            pltpu.VMEM((chunks, rays // LANES, 16 * samples, LANES), f32),
            pltpu.VMEM((chunks, 5, samples, rays), f32),
            pltpu.VMEM((chunks, 5, hid, rays), f32),
            pltpu.VMEM((chunks, 8, LANES), f32),
            pltpu.VMEM((n_slab, chunks, 8, LANES), f32),
            pltpu.VMEM((enc, hid), f32),
            pltpu.VMEM((hid, enc), f32),
            pltpu.VMEM((hid, hid), f32),
            pltpu.VMEM((out, hid), f32),
            *(pltpu.VMEM((r // 2, n), f32) for r, n in sizes),
            *(pltpu.VMEM((r // 2, n), f32) for r, n in sizes),
            *(pltpu.VMEM((2, r // 2, n), f32) for r, n in sizes),
            *(pltpu.VMEM((2, r // 2, n), f32) for r, n in sizes),
            *(pltpu.VMEM((r // 2, n), f32) for r, n in sizes[::2]),
            pltpu.VMEM((hid // 2, hid), f32),
            pltpu.SemaphoreType.DMA((chunks + 10,)),
            pltpu.SemaphoreType.DMA((n_slab,)),
            pltpu.SemaphoreType.DMA((n_slab,)),
            pltpu.SemaphoreType.DMA((3,)),
            pltpu.SemaphoreType.DMA((3,)),
            pltpu.SemaphoreType.DMA((3, 2, 2, 2)),
            pltpu.SemaphoreType.DMA((3, 2, 2, 2)),
            pltpu.SemaphoreType.DMA((3,)),
            pltpu.SemaphoreType.DMA((3,)),
        ]
        shapes = (
            jax.ShapeDtypeStruct((1, rays_dev), f32),
            jax.ShapeDtypeStruct((enc, hid), f32),
            jax.ShapeDtypeStruct((hid, hid), f32),
            jax.ShapeDtypeStruct((out, hid), f32),
        )
        results = pl.pallas_call(
            functools.partial(kernel, chunks, n_slab, n_tile),
            out_shape=tuple(pltpu.VMEM(q.shape, q.dtype) for q in shapes),
            in_specs=[any_space] * 11,
            out_specs=(vmem,) * 4,
            scratch_shapes=scratch,
            compiler_params=pltpu.CompilerParams(
                collective_id=0, has_side_effects=True, vmem_limit_bytes=56 * 2**20
            ),
        )(
            encoded,
            spacing,
            counts,
            row(seg_first),
            row(seg_last),
            row(direction),
            field_in,
            field_mid,
            field_out.transpose(0, 2, 1),
            color_head.T,
            target.T,
        )
        front, g1, g2, g3t = pl.pallas_call(
            hand_on,
            out_shape=shapes,
            in_specs=[vmem] * 4,
            out_specs=(vmem,) * 4,
        )(*(pltpu.with_memory_space_constraint(r, pltpu.VMEM) for r in results))
        return front, g1[None], g2[None], g3t.T[None]

    return jax.shard_map(
        body,
        mesh=mesh,
        in_specs=(
            P("slab", None, "tile", None),
            P("slab", None, "tile"),
            P("slab", "tile"),
            P("tile"),
            P("tile"),
            P("tile"),
            P("slab", None, None),
            P("slab", None, None),
            P("slab", None, None),
            P(),
            P("tile", None),
        ),
        out_specs=(
            P("slab", "tile"),
            P("slab", None, None),
            P("slab", None, None),
            P("slab", None, None),
        ),
        check_vma=False,
    )
```

```python
import functools
import math

import jax
import jax.numpy as jnp
from jax import lax
from jax.experimental import pallas as pl
from jax.experimental.pallas import tpu as pltpu
from jax.sharding import PartitionSpec as P

MESH = pl.DeviceIdType.MESH
NN = ((1,), (0,))
NT = ((1,), (1,))
LANES = 128


def mm(a, b, dims):
    return lax.dot_general(a, b, (dims, ((), ())), preferred_element_type=jnp.float32)


def running_sum(values):
    rows = values.shape[0]
    row_ids = lax.broadcasted_iota(jnp.int32, values.shape, 0)
    shift = 1
    while shift < rows:
        moved = pltpu.roll(values, shift, axis=0)
        values = values + jnp.where(row_ids >= shift, moved, 0.0)
        shift *= 2
    return values


def kernel(
    chunks,
    n_slab,
    n_tile,
    x_hbm,
    space_hbm,
    counts_hbm,
    first_hbm,
    last_hbm,
    dir_hbm,
    w1_hbm,
    w2_hbm,
    w3t_hbm,
    head_hbm,
    target_hbm,
    front_out,
    g1_out,
    g2_out,
    g3_out,
    x_s,
    space_s,
    ints_s,
    w1_s,
    w2_s,
    w3t_s,
    head_s,
    target_s,
    w1t_s,
    w2t_s,
    head8_s,
    headt_s,
    w3p_s,
    fold_s,
    foldt_s,
    h1_s,
    h2_s,
    b2_s,
    coef_s,
    proj_s,
    stack_s,
    saved_s,
    held_s,
    send_s,
    gather_s,
    g1_s,
    g1t_s,
    g2_s,
    g3_s,
    pair1_s,
    pair2_s,
    pair3_s,
    mid1_s,
    mid2_s,
    mid3_s,
    near1_s,
    near2_s,
    near3_s,
    far1_s,
    far2_s,
    far3_s,
    other1_s,
    other3_s,
    half2_s,
    in_sem,
    ex_send,
    ex_recv,
    pair_send,
    pair_recv,
    swap_send,
    swap_recv,
    pass_send,
    pass_recv,
):
    samples, rays_dev = space_s.shape
    rays = rays_dev // chunks
    cols = samples * rays
    groups = rays // LANES
    me = lax.axis_index("slab")
    tile = lax.axis_index("tile")
    core, ypos = tile % 2, tile // 2
    n_y = n_tile // 2

    small = [
        (w1_hbm.at[0], w1_s),
        (w2_hbm.at[0], w2_s),
        (w3t_hbm.at[0], w3t_s),
        (head_hbm, head_s),
        (space_hbm.at[0], space_s),
        (counts_hbm, ints_s.at[0]),
        (first_hbm, ints_s.at[1]),
        (last_hbm, ints_s.at[2]),
        (dir_hbm, ints_s.at[3]),
        (target_hbm, target_s),
    ]
    loads = [
        pltpu.make_async_copy(src, dst, in_sem.at[chunks + i]) for i, (src, dst) in enumerate(small)
    ]
    x_loads = [
        pltpu.make_async_copy(
            x_hbm.at[0, :, pl.ds(c * rays, rays), :], x_s.at[c], in_sem.at[c]
        )
        for c in range(chunks)
    ]
    loads[0].start()
    x_loads[0].start()
    for load in loads[1:]:
        load.start()
    for load in x_loads[1:]:
        load.start()

    barrier = pltpu.get_barrier_semaphore()
    for step in range(1, n_slab):
        pl.semaphore_signal(
            barrier, inc=1, device_id={"slab": (me + step) % n_slab}, device_id_type=MESH
        )
    across = (ypos + 1 - 2 * (ypos % 2), n_y - 1 - ypos)
    mates = [ypos * 2 + 1 - core] + [y * 2 + c for y in across for c in (core, 1 - core)]
    for mate in mates:
        pl.semaphore_signal(barrier, inc=1, device_id={"tile": mate}, device_id_type=MESH)

    loads[0].wait()
    w1t_s[...] = w1_s[...].T
    loads[1].wait()
    w2t_s[...] = w2_s[...].T
    loads[2].wait()
    loads[3].wait()
    head8_s[...] = jnp.zeros_like(head8_s)
    lane = lax.broadcasted_iota(jnp.int32, (1, LANES), 1)
    head8_s[0:1, :] = (lane == 0).astype(jnp.float32)
    head8_s[1:4, 0 : head_s.shape[1]] = head_s[...]
    headt_s[...] = head8_s[...].T
    width = w3t_s.shape[0]
    folded = lax.dot_general(
        head8_s[:, 0:width],
        w3t_s[...].astype(jnp.float32),
        (NN, ((), ())),
        precision=lax.Precision.HIGHEST,
        preferred_element_type=jnp.float32,
    )
    hi = folded.astype(jnp.bfloat16).astype(jnp.float32)
    mid = (folded - hi).astype(jnp.bfloat16).astype(jnp.float32)
    low = folded - hi - mid
    zeros = jnp.zeros_like(folded)
    w3p_s[...] = jnp.concatenate([hi, mid, low, zeros], axis=0).astype(jnp.bfloat16)
    fold_s[...] = jnp.zeros_like(fold_s)
    fold_s[0:4, :] = hi[0:4]
    fold_s[4:8, :] = hi[0:4]
    fold_s[8:12, :] = mid[0:4]
    foldt_s[...] = fold_s[...].T[:, 0:16].astype(jnp.bfloat16)
    stack_s[...] = jnp.zeros_like(stack_s)
    for load in loads[4:]:
        load.wait()

    row_ids = lax.broadcasted_iota(jnp.int32, (samples, rays), 0)
    tile_rows = lax.broadcasted_iota(jnp.int32, (8, LANES), 0)
    is_trans = (tile_rows % 4) == 0
    identity = is_trans.astype(jnp.float32)

    def spread(v):
        return jnp.where(tile_rows < 4, v[0:1, :], v[4:5, :])

    def ray_slice(c):
        return pl.ds(c * rays, rays)

    side = math.isqrt(n_slab)
    near = lambda d: min(d, side - d)
    moves = sorted(
        ((dx, dz) for dx in range(side) for dz in range(side) if dx or dz),
        key=lambda d: -near(d[0]) - near(d[1]),
    )

    def slab_at(dx, dz):
        return (me // side + dx) % side * side + (me % side + dz) % side

    def exchange(step, source):
        return pltpu.make_async_remote_copy(
            src_ref=send_s,
            dst_ref=gather_s.at[source],
            send_sem=ex_send.at[step],
            recv_sem=ex_recv.at[source],
            device_id={"slab": slab_at(*moves[step])},
            device_id_type=MESH,
        )

    def origin(step):
        dx, dz = moves[step]
        return slab_at(side - dx, side - dz)

    def lanes_of(values, g):
        return values[:, g * LANES : (g + 1) * LANES]

    def later_sum(values, reverse):
        running = running_sum(values)
        return jnp.where(reverse, running - values, running[samples - 1 : samples, :] - running)

    def forward_samples(c):
        x_loads[c].wait()
        x = x_s[c].reshape(cols, x_s.shape[3])
        base = c * cols
        h1 = jnp.maximum(mm(w1t_s[...], x, NT).astype(jnp.bfloat16), 0)
        h1_s[:, pl.ds(base, cols)] = h1
        h2 = jnp.maximum(mm(w2t_s[...], h1, NN).astype(jnp.bfloat16), 0)
        h2_s[:, pl.ds(base, cols)] = h2
        p = mm(w3p_s[...], h2, NN)
        p = p[0:8, :] + (p[8:16, :] + p[16:24, :])
        for j in range(samples):
            for g in range(groups):
                at = j * rays + g * LANES
                proj_s[c, g, 8 * j : 8 * j + 8, :] = p[:, at : at + LANES]

    def forward_rays(c):
        o0, *ps = (
            jnp.concatenate(
                [proj_s[c, g, pl.ds(k, samples, stride=8), :] for g in range(groups)], 1
            )
            for k in range(4)
        )
        rs = ray_slice(c)
        counts = ints_s[0, :, rs]
        first = ints_s[1, :, rs]
        last = ints_s[2, :, rs]
        reverse = ints_s[3, :, rs] > 0
        active = (first <= me) & (me < last)
        live = ((row_ids < counts) & active).astype(jnp.float32)
        span = space_s[:, rs] * live
        soft = jnp.maximum(o0, 0.0) + jnp.log1p(jnp.exp(-jnp.abs(o0)))
        optical = soft * span
        running = running_sum(optical)
        column = running[samples - 1 : samples, :]
        before = jnp.where(reverse, column - running, running - optical)
        gone = jnp.exp(-before)
        stay = jnp.exp(-optical)
        weights = gone * (1.0 - stay)
        trans = jnp.exp(-column)
        shown = [weights * ps[k] for k in range(3)]
        rows = [trans] + [jnp.sum(shown[k], axis=0, keepdims=True) for k in range(3)]
        for g in range(groups):
            for k in range(4):
                send_s[c, 4 * g + k : 4 * g + k + 1, :] = lanes_of(rows[k], g)
        return o0, ps, span, gone * stay, weights, shown, trans, reverse

    def slopes(c, values):
        o0, ps, span, spent, weights, shown, trans, reverse = values
        slope = span * (1.0 / (1.0 + jnp.exp(-o0)))
        saved_s[c, 0] = weights
        for k in range(3):
            saved_s[c, 1 + k] = slope * (spent * ps[k] - later_sum(shown[k], reverse))
        saved_s[c, 4] = -(trans * slope)

    def hold(c):
        base = c * cols
        block = 32
        for f in range(0, h2_s.shape[0], block):
            sums = [None] * 5
            for j in range(samples):
                h2 = h2_s[f : f + block, pl.ds(base + j * rays, rays)].astype(jnp.float32)
                for m in range(5):
                    term = h2 * saved_s[c, m, j : j + 1, :]
                    sums[m] = term if j == 0 else sums[m] + term
            for m in range(5):
                held_s[c, m, f : f + block, :] = sums[m]

    def compose(c):
        rs = ray_slice(c)
        rev = jnp.where(
            tile_rows < 4,
            jnp.broadcast_to(ints_s[3, :, pl.ds(c * rays, LANES)], (8, LANES)),
            jnp.broadcast_to(ints_s[3, :, pl.ds(c * rays + (groups - 1) * LANES, LANES)], (8, LANES)),
        ) > 0

        def step_of(pair, item, item_first):
            run, run_t = pair
            item_t = spread(item)
            run_first = jnp.where(is_trans, 0.0, run) + run_t * item
            late_first = jnp.where(is_trans, 0.0, item) + item_t * run
            return jnp.where(item_first, late_first, run_first), run_t * item_t

        low = high = (identity, jnp.ones_like(identity))
        for s in range(n_slab):
            t = n_slab - 1 - s
            low = step_of(low, jnp.where(s < me, gather_s[s, c], identity), rev)
            high = step_of(high, jnp.where(t > me, gather_s[t, c], identity), jnp.logical_not(rev))
        low, low_t = low
        high, high_t = high
        own = send_s[c]
        front = jnp.where(rev, high, low)
        back = jnp.where(rev, low, high)
        front_t, own_t = jnp.where(rev, high_t, low_t), spread(own)
        logits = front + front_t * own + (front_t * own_t) * back
        shade = 1.0 / (1.0 + jnp.exp(-logits))
        target = jnp.zeros((8, LANES), jnp.float32)
        for g in range(groups):
            for k in range(3):
                target = jnp.where(
                    tile_rows == 4 * g + 1 + k,
                    target_s[k : k + 1, pl.ds(c * rays + g * LANES, LANES)],
                    target,
                )
        grad3 = jnp.where(is_trans, 0.0, (shade - target) * (1.0 / rays_dev) * shade * (1.0 - shade))
        seg = front_t * grad3
        dots = seg * back
        fronts, grads, seg_t = [], [[], [], []], []
        for g in range(groups):
            r = 4 * g
            fronts.append(front[r : r + 1, :])
            for k in range(3):
                grads[k].append(seg[r + 1 + k : r + 2 + k, :])
            seg_t.append(dots[r + 1 : r + 2, :] + dots[r + 2 : r + 3, :] + dots[r + 3 : r + 4, :])
        join = lambda parts: jnp.concatenate(parts, 1)
        front_out[:, rs] = join(fronts)
        return [join(grads[k]) for k in range(3)] + [join(seg_t)]

    def coefficients(c, cot):
        weights = saved_s[c, 0]
        density = (
            cot[0] * saved_s[c, 1] + cot[1] * saved_s[c, 2] + cot[2] * saved_s[c, 3] + cot[3] * saved_s[c, 4]
        )
        for m, value in enumerate([density] + [cot[k] * weights for k in range(3)]):
            hi = value.astype(jnp.bfloat16).astype(jnp.float32)
            for g in range(groups):
                for row, part in ((m, hi), (4 + m, value - hi), (8 + m, hi)):
                    stack_s[c, g, row * samples : (row + 1) * samples, :] = lanes_of(part, g)
        for j in range(samples):
            for g in range(groups):
                coef_s[:, pl.ds(c * cols + j * rays + g * LANES, LANES)] = jnp.concatenate(
                    [
                        stack_s[c, g, pl.ds(j, 8, stride=samples), :],
                        stack_s[c, g, pl.ds(8 * samples + j, 8, stride=samples), :],
                    ],
                    0,
                ).astype(jnp.bfloat16)

    def grad_out(cots):
        hid = h2_s.shape[0]
        block = 32
        column = lax.broadcasted_iota(jnp.int32, (block, LANES), 1)
        for f in range(0, hid, block):
            parts = [0.0] * 4
            for c in range(chunks):
                for g in range(groups):
                    at = pl.ds(g * LANES, LANES)
                    shown = held_s[c, 0, f : f + block, at]
                    for k in range(3):
                        parts[k] = parts[k] + shown * lanes_of(cots[c][k], g)
                    for m in range(4):
                        parts[3] = parts[3] + held_s[c, 1 + m, f : f + block, at] * lanes_of(cots[c][m], g)
            packed = jnp.zeros((block, LANES), jnp.float32)
            for k in range(4):
                packed = jnp.where(column == k, jnp.sum(parts[k], axis=1, keepdims=True), packed)
            held_s[0, 0, f : f + block, 0:LANES] = packed
        sums = held_s[0, 0, :, 0:LANES].T
        first_row = lax.broadcasted_iota(jnp.int32, (width, 1), 0) == 0
        total = jnp.where(first_row, sums[3:4, :], 0.0)
        for k in range(3):
            total = total + headt_s[0:width, 1 + k : 2 + k] * sums[k : k + 1, :]
        g3_s[...] = total

    def backward_two(c):
        base = c * cols
        b2 = mm(foldt_s[...], coef_s[:, pl.ds(base, cols)], NN).astype(jnp.bfloat16)
        b2 = jnp.where(h2_s[:, pl.ds(base, cols)] > 0, b2, 0)
        b2_s[:, pl.ds(base, cols)] = b2
        part = mm(h1_s[:, pl.ds(base, cols)], b2, NT)
        g2_s[...] = part if c == 0 else g2_s[...] + part

    def backward_one(c):
        base = c * cols
        b1 = mm(w2_s[...], b2_s[:, pl.ds(base, cols)], NN).astype(jnp.bfloat16)
        b1 = jnp.where(h1_s[:, pl.ds(base, cols)] > 0, b1, 0)
        part = mm(b1, x_s[c].reshape(cols, x_s.shape[3]), NN)
        g1t_s[...] = part if c == 0 else g1t_s[...] + part

    grads = (
        (g1_s, pair1_s, near1_s, mid1_s, far1_s, other1_s, g1_out),
        (g2_s, pair2_s, near2_s, mid2_s, far2_s, None, g2_out),
        (g3_s, pair3_s, near3_s, mid3_s, far3_s, other3_s, g3_out),
    )
    partner = ypos * 2 + 1 - core

    def half_rows(i, k):
        rows = grads[i][1].shape[0]
        return pl.ds(pl.multiple_of(k * rows, 8), rows)

    def part_rows(i, part):
        rows = grads[i][1].shape[0] // 2
        return pl.ds(part * rows, rows)

    def pair_copy(i):
        whole, pair = grads[i][:2]
        return pltpu.make_async_remote_copy(
            src_ref=whole.at[half_rows(i, 1 - core), :],
            dst_ref=pair,
            send_sem=pair_send.at[i],
            recv_sem=pair_recv.at[i],
            device_id={"tile": partner},
            device_id_type=MESH,
        )

    def swap_copy(i, stage, part, turn):
        whole, pair, near, mid, far = grads[i][:5]
        rows = pair.shape[0] // 2
        if stage == 0 and i == 1:
            source, target = half2_s.at[part_rows(i, part), :], near
        elif stage == 0:
            half = 1 - core if turn else core
            at = pl.multiple_of(half * (2 * rows) + part * rows, 8)
            source, target = whole.at[pl.ds(at, rows), :], near
        else:
            source, target = mid.at[part_rows(i, part), :], far
        return pltpu.make_async_remote_copy(
            src_ref=source,
            dst_ref=target.at[turn, part_rows(i, part), :],
            send_sem=swap_send.at[i, stage, part, turn],
            recv_sem=swap_recv.at[i, stage, part, turn],
            device_id={"tile": across[(stage + part) % 2] * 2 + (1 - core if turn else core)},
            device_id_type=MESH,
        )

    def pass_copy(i):
        source, target = grads[i][3], grads[i][5]
        if i == 1:
            source = target = g2_out.at[half_rows(1, core), :]
        return pltpu.make_async_remote_copy(
            src_ref=source,
            dst_ref=target,
            send_sem=pass_send.at[i],
            recv_sem=pass_recv.at[i],
            device_id={"tile": partner},
            device_id_type=MESH,
        )

    def send_own(i):
        for turn in range(2):
            for part in range(2):
                swap_copy(i, 0, part, turn).start()
        pair_copy(i).start()

    def send_sums(i):
        whole, pair, near, mid = grads[i][:4]
        rows = pair.shape[0] // 2
        pair_copy(i).wait_recv()
        for part in range(2):
            for turn in range(2):
                swap_copy(i, 0, part, turn).wait_recv()
            at = part_rows(i, part)
            own = whole[pl.ds(pl.multiple_of(core * (2 * rows) + part * rows, 8), rows), :]
            mid[at, :] = (own + pair[at, :]) + (near[0, at, :] + near[1, at, :])
            for turn in range(2):
                swap_copy(i, 1, part, turn).start()
        pass_copy(i).start()

    def lean_first():
        pair_copy(1).wait_recv()
        half2_s[...] = g2_s[half_rows(1, core), :] + pair2_s[...]
        for part in range(2):
            swap_copy(1, 0, part, 0).start()

    def lean_second():
        for part in range(2):
            swap_copy(1, 0, part, 0).wait_recv()
            at = part_rows(1, part)
            mid2_s[at, :] = half2_s[at, :] + near2_s[0, at, :]
            swap_copy(1, 1, part, 0).start()

    def lean_third():
        for part in range(2):
            swap_copy(1, 1, part, 0).wait_recv()
        g2_out[half_rows(1, core), :] = mid2_s[...] + far2_s[0]
        pass_copy(1).start()

    def finish(i):
        mid, far, other, out = grads[i][3:]
        for turn in range(2):
            for part in range(2):
                swap_copy(i, 1, part, turn).wait_recv()
        out[half_rows(i, core), :] = mid[...] + far[0]
        pass_copy(i).wait_recv()
        out[half_rows(i, 1 - core), :] = other[...] + far[1]

    for c in range(chunks):
        forward_samples(c)
    values = [forward_rays(c) for c in range(chunks)]
    pl.semaphore_wait(barrier, n_slab - 1 + len(mates))
    for step in range(n_slab - 1):
        exchange(step, me).start()
    gather_s[me] = send_s[...]
    for c in range(chunks):
        slopes(c, values[c])
    for c in range(chunks):
        hold(c)
    for step in range(n_slab - 1):
        exchange(step, origin(step)).wait_recv()
    cots = [compose(c) for c in range(chunks)]
    coefficients(0, cots[0])
    backward_two(0)
    coefficients(1, cots[1])
    grad_out(cots)
    send_own(2)
    backward_two(1)
    pair_copy(1).start()
    backward_one(0)
    lean_first()
    backward_one(1)
    g1_s[...] = g1t_s[...].T
    send_own(0)
    send_sums(2)
    lean_second()
    send_sums(0)
    finish(2)
    lean_third()
    finish(0)
    pass_copy(1).wait_recv()
    for i in (2, 1, 0):
        pass_copy(i).wait_send()
        pair_copy(i).wait_send()
        for stage in range(2):
            for part in range(2):
                for turn in range(1 if i == 1 else 2):
                    swap_copy(i, stage, part, turn).wait_send()
    for step in range(n_slab - 1):
        exchange(step, me).wait_send()


def hand_on(*refs):
    half = len(refs) // 2
    for src, dst in zip(refs[:half], refs[half:]):
        dst[...] = src[...]


def solution(mesh):
    n_slab, n_tile = mesh.shape["slab"], mesh.shape["tile"]
    chunks = 2

    def body(
        encoded,
        spacing,
        counts,
        seg_first,
        seg_last,
        direction,
        field_in,
        field_mid,
        field_out,
        color_head,
        target,
    ):
        _, samples, rays_dev, enc = encoded.shape
        hid, out = field_out.shape[1:]
        rays = rays_dev // chunks
        total = samples * rays_dev
        f32, bf16 = jnp.float32, jnp.bfloat16
        row = lambda v: v.reshape(1, rays_dev)
        sizes = ((enc, hid), (hid, hid), (out, hid))
        any_space = pl.BlockSpec(memory_space=pl.ANY)
        vmem = pl.BlockSpec(memory_space=pltpu.VMEM)
        scratch = [
            pltpu.VMEM((chunks, samples, rays, enc), bf16),
            pltpu.VMEM((samples, rays_dev), f32),
            pltpu.VMEM((4, 1, rays_dev), jnp.int32),
            pltpu.VMEM((enc, hid), bf16),
            pltpu.VMEM((hid, hid), bf16),
            pltpu.VMEM((out, hid), bf16),
            pltpu.VMEM((3, out), f32),
            pltpu.VMEM((3, rays_dev), f32),
            pltpu.VMEM((hid, enc), bf16),
            pltpu.VMEM((hid, hid), bf16),
            pltpu.VMEM((8, LANES), f32),
            pltpu.VMEM((LANES, 8), f32),
            pltpu.VMEM((32, hid), bf16),
            pltpu.VMEM((LANES, hid), f32),
            pltpu.VMEM((hid, 16), bf16),
            pltpu.VMEM((hid, total), bf16),
            pltpu.VMEM((hid, total), bf16),
            pltpu.VMEM((hid, total), bf16),
            pltpu.VMEM((16, total), bf16),
            pltpu.VMEM((chunks, rays // LANES, 8 * samples, LANES), f32),
            pltpu.VMEM((chunks, rays // LANES, 16 * samples, LANES), f32),
            pltpu.VMEM((chunks, 5, samples, rays), f32),
            pltpu.VMEM((chunks, 5, hid, rays), f32),
            pltpu.VMEM((chunks, 8, LANES), f32),
            pltpu.VMEM((n_slab, chunks, 8, LANES), f32),
            pltpu.VMEM((enc, hid), f32),
            pltpu.VMEM((hid, enc), f32),
            pltpu.VMEM((hid, hid), f32),
            pltpu.VMEM((out, hid), f32),
            *(pltpu.VMEM((r // 2, n), f32) for r, n in sizes),
            *(pltpu.VMEM((r // 2, n), f32) for r, n in sizes),
            *(pltpu.VMEM((2, r // 2, n), f32) for r, n in sizes),
            *(pltpu.VMEM((2, r // 2, n), f32) for r, n in sizes),
            *(pltpu.VMEM((r // 2, n), f32) for r, n in sizes[::2]),
            pltpu.VMEM((hid // 2, hid), f32),
            pltpu.SemaphoreType.DMA((chunks + 10,)),
            pltpu.SemaphoreType.DMA((n_slab,)),
            pltpu.SemaphoreType.DMA((n_slab,)),
            pltpu.SemaphoreType.DMA((3,)),
            pltpu.SemaphoreType.DMA((3,)),
            pltpu.SemaphoreType.DMA((3, 2, 2, 2)),
            pltpu.SemaphoreType.DMA((3, 2, 2, 2)),
            pltpu.SemaphoreType.DMA((3,)),
            pltpu.SemaphoreType.DMA((3,)),
        ]
        shapes = (
            jax.ShapeDtypeStruct((1, rays_dev), f32),
            jax.ShapeDtypeStruct((enc, hid), f32),
            jax.ShapeDtypeStruct((hid, hid), f32),
            jax.ShapeDtypeStruct((out, hid), f32),
        )
        results = pl.pallas_call(
            functools.partial(kernel, chunks, n_slab, n_tile),
            out_shape=tuple(pltpu.VMEM(q.shape, q.dtype) for q in shapes),
            in_specs=[any_space] * 11,
            out_specs=(vmem,) * 4,
            scratch_shapes=scratch,
            compiler_params=pltpu.CompilerParams(
                collective_id=0, has_side_effects=True, vmem_limit_bytes=56 * 2**20
            ),
        )(
            encoded,
            spacing,
            counts,
            row(seg_first),
            row(seg_last),
            row(direction),
            field_in,
            field_mid,
            field_out.transpose(0, 2, 1),
            color_head.T,
            target.T,
        )
        front, g1, g2, g3t = pl.pallas_call(
            hand_on,
            out_shape=shapes,
            in_specs=[vmem] * 4,
            out_specs=(vmem,) * 4,
        )(*(pltpu.with_memory_space_constraint(r, pltpu.VMEM) for r in results))
        return front, g1[None], g2[None], g3t.T[None]

    return jax.shard_map(
        body,
        mesh=mesh,
        in_specs=(
            P("slab", None, "tile", None),
            P("slab", None, "tile"),
            P("slab", "tile"),
            P("tile"),
            P("tile"),
            P("tile"),
            P("slab", None, None),
            P("slab", None, None),
            P("slab", None, None),
            P(),
            P("tile", None),
        ),
        out_specs=(
            P("slab", "tile"),
            P("slab", None, None),
            P("slab", None, None),
            P("slab", None, None),
        ),
        check_vma=False,
    )
```

```python
import functools
import math

import jax
import jax.numpy as jnp
from jax import lax
from jax.experimental import pallas as pl
from jax.experimental.pallas import tpu as pltpu
from jax.sharding import PartitionSpec as P

MESH = pl.DeviceIdType.MESH
NN = ((1,), (0,))
NT = ((1,), (1,))
LANES = 128


def mm(a, b, dims):
    return lax.dot_general(a, b, (dims, ((), ())), preferred_element_type=jnp.float32)


def running_sum(values):
    rows = values.shape[0]
    row_ids = lax.broadcasted_iota(jnp.int32, values.shape, 0)
    shift = 1
    while shift < rows:
        moved = pltpu.roll(values, shift, axis=0)
        values = values + jnp.where(row_ids >= shift, moved, 0.0)
        shift *= 2
    return values


def kernel(
    chunks,
    n_slab,
    n_tile,
    x_hbm,
    space_hbm,
    counts_hbm,
    first_hbm,
    last_hbm,
    dir_hbm,
    w1_hbm,
    w2_hbm,
    w3t_hbm,
    head_hbm,
    target_hbm,
    front_out,
    g1_out,
    g2_out,
    g3_out,
    x_s,
    space_s,
    ints_s,
    w1_s,
    w2_s,
    w3t_s,
    head_s,
    target_s,
    w1t_s,
    w2t_s,
    head8_s,
    headt_s,
    w3p_s,
    fold_s,
    foldt_s,
    h1_s,
    h2_s,
    b2_s,
    coef_s,
    proj_s,
    stack_s,
    saved_s,
    held_s,
    send_s,
    gather_s,
    g1_s,
    g2_s,
    g3_s,
    pair1_s,
    pair2_s,
    pair3_s,
    mid1_s,
    mid2_s,
    mid3_s,
    near1_s,
    near2_s,
    near3_s,
    far1_s,
    far2_s,
    far3_s,
    other1_s,
    other3_s,
    half2_s,
    in_sem,
    ex_send,
    ex_recv,
    pair_send,
    pair_recv,
    swap_send,
    swap_recv,
    pass_send,
    pass_recv,
):
    samples, rays_dev = space_s.shape
    rays = rays_dev // chunks
    cols = samples * rays
    groups = rays // LANES
    me = lax.axis_index("slab")
    tile = lax.axis_index("tile")
    core, ypos = tile % 2, tile // 2
    n_y = n_tile // 2

    small = [
        (w1_hbm.at[0], w1_s),
        (w2_hbm.at[0], w2_s),
        (w3t_hbm.at[0], w3t_s),
        (head_hbm, head_s),
        (space_hbm.at[0], space_s),
        (counts_hbm, ints_s.at[0]),
        (first_hbm, ints_s.at[1]),
        (last_hbm, ints_s.at[2]),
        (dir_hbm, ints_s.at[3]),
        (target_hbm, target_s),
    ]
    loads = [
        pltpu.make_async_copy(src, dst, in_sem.at[chunks + i]) for i, (src, dst) in enumerate(small)
    ]
    x_loads = [
        pltpu.make_async_copy(
            x_hbm.at[0, :, pl.ds(c * rays, rays), :], x_s.at[c], in_sem.at[c]
        )
        for c in range(chunks)
    ]
    loads[0].start()
    x_loads[0].start()
    for load in loads[1:]:
        load.start()
    for load in x_loads[1:]:
        load.start()

    barrier = pltpu.get_barrier_semaphore()
    for step in range(1, n_slab):
        pl.semaphore_signal(
            barrier, inc=1, device_id={"slab": (me + step) % n_slab}, device_id_type=MESH
        )
    across = (ypos + 1 - 2 * (ypos % 2), n_y - 1 - ypos)
    mates = [ypos * 2 + 1 - core] + [y * 2 + c for y in across for c in (core, 1 - core)]
    for mate in mates:
        pl.semaphore_signal(barrier, inc=1, device_id={"tile": mate}, device_id_type=MESH)

    loads[0].wait()
    w1t_s[...] = w1_s[...].T
    loads[1].wait()
    w2t_s[...] = w2_s[...].T
    loads[2].wait()
    loads[3].wait()
    head8_s[...] = jnp.zeros_like(head8_s)
    lane = lax.broadcasted_iota(jnp.int32, (1, LANES), 1)
    head8_s[0:1, :] = (lane == 0).astype(jnp.float32)
    head8_s[1:4, 0 : head_s.shape[1]] = head_s[...]
    headt_s[...] = head8_s[...].T
    width = w3t_s.shape[0]
    folded = lax.dot_general(
        head8_s[:, 0:width],
        w3t_s[...].astype(jnp.float32),
        (NN, ((), ())),
        precision=lax.Precision.HIGHEST,
        preferred_element_type=jnp.float32,
    )
    hi = folded.astype(jnp.bfloat16).astype(jnp.float32)
    mid = (folded - hi).astype(jnp.bfloat16).astype(jnp.float32)
    low = folded - hi - mid
    zeros = jnp.zeros_like(folded)
    w3p_s[...] = jnp.concatenate([hi, mid, low, zeros], axis=0).astype(jnp.bfloat16)
    fold_s[...] = jnp.zeros_like(fold_s)
    fold_s[0:4, :] = hi[0:4]
    fold_s[4:8, :] = hi[0:4]
    fold_s[8:12, :] = mid[0:4]
    foldt_s[...] = fold_s[...].T[:, 0:16].astype(jnp.bfloat16)
    stack_s[...] = jnp.zeros_like(stack_s)
    for load in loads[4:]:
        load.wait()

    row_ids = lax.broadcasted_iota(jnp.int32, (samples, rays), 0)
    tile_rows = lax.broadcasted_iota(jnp.int32, (8, LANES), 0)
    is_trans = (tile_rows % 4) == 0
    identity = is_trans.astype(jnp.float32)

    def spread(v):
        return jnp.where(tile_rows < 4, v[0:1, :], v[4:5, :])

    def ray_slice(c):
        return pl.ds(c * rays, rays)

    side = math.isqrt(n_slab)
    near = lambda d: min(d, side - d)
    moves = sorted(
        ((dx, dz) for dx in range(side) for dz in range(side) if dx or dz),
        key=lambda d: -near(d[0]) - near(d[1]),
    )

    def slab_at(dx, dz):
        return (me // side + dx) % side * side + (me % side + dz) % side

    def exchange(step, source):
        return pltpu.make_async_remote_copy(
            src_ref=send_s,
            dst_ref=gather_s.at[source],
            send_sem=ex_send.at[step],
            recv_sem=ex_recv.at[source],
            device_id={"slab": slab_at(*moves[step])},
            device_id_type=MESH,
        )

    def origin(step):
        dx, dz = moves[step]
        return slab_at(side - dx, side - dz)

    def lanes_of(values, g):
        return values[:, g * LANES : (g + 1) * LANES]

    def later_sum(values, reverse):
        running = running_sum(values)
        return jnp.where(reverse, running - values, running[samples - 1 : samples, :] - running)

    def forward_samples(c):
        x_loads[c].wait()
        x = x_s[c].reshape(cols, x_s.shape[3])
        base = c * cols
        h1 = jnp.maximum(mm(w1t_s[...], x, NT).astype(jnp.bfloat16), 0)
        h1_s[:, pl.ds(base, cols)] = h1
        h2 = jnp.maximum(mm(w2t_s[...], h1, NN).astype(jnp.bfloat16), 0)
        h2_s[:, pl.ds(base, cols)] = h2
        p = mm(w3p_s[...], h2, NN)
        p = p[0:8, :] + (p[8:16, :] + p[16:24, :])
        for j in range(samples):
            for g in range(groups):
                at = j * rays + g * LANES
                proj_s[c, g, 8 * j : 8 * j + 8, :] = p[:, at : at + LANES]

    def forward_rays(c):
        o0, *ps = (
            jnp.concatenate(
                [proj_s[c, g, pl.ds(k, samples, stride=8), :] for g in range(groups)], 1
            )
            for k in range(4)
        )
        rs = ray_slice(c)
        counts = ints_s[0, :, rs]
        first = ints_s[1, :, rs]
        last = ints_s[2, :, rs]
        reverse = ints_s[3, :, rs] > 0
        active = (first <= me) & (me < last)
        live = ((row_ids < counts) & active).astype(jnp.float32)
        span = space_s[:, rs] * live
        soft = jnp.maximum(o0, 0.0) + jnp.log1p(jnp.exp(-jnp.abs(o0)))
        optical = soft * span
        running = running_sum(optical)
        column = running[samples - 1 : samples, :]
        before = jnp.where(reverse, column - running, running - optical)
        gone = jnp.exp(-before)
        stay = jnp.exp(-optical)
        weights = gone * (1.0 - stay)
        trans = jnp.exp(-column)
        shown = [weights * ps[k] for k in range(3)]
        rows = [trans] + [jnp.sum(shown[k], axis=0, keepdims=True) for k in range(3)]
        for g in range(groups):
            for k in range(4):
                send_s[c, 4 * g + k : 4 * g + k + 1, :] = lanes_of(rows[k], g)
        return o0, ps, span, gone * stay, weights, shown, trans, reverse

    def slopes(c, values):
        o0, ps, span, spent, weights, shown, trans, reverse = values
        slope = span * (1.0 / (1.0 + jnp.exp(-o0)))
        saved_s[c, 0] = weights
        for k in range(3):
            saved_s[c, 1 + k] = slope * (spent * ps[k] - later_sum(shown[k], reverse))
        saved_s[c, 4] = -(trans * slope)

    def hold(c):
        base = c * cols
        block = 32
        for f in range(0, h2_s.shape[0], block):
            sums = [None] * 5
            for j in range(samples):
                h2 = h2_s[f : f + block, pl.ds(base + j * rays, rays)].astype(jnp.float32)
                for m in range(5):
                    term = h2 * saved_s[c, m, j : j + 1, :]
                    sums[m] = term if j == 0 else sums[m] + term
            for m in range(5):
                held_s[c, m, f : f + block, :] = sums[m]

    def compose(c):
        rs = ray_slice(c)
        rev = jnp.where(
            tile_rows < 4,
            jnp.broadcast_to(ints_s[3, :, pl.ds(c * rays, LANES)], (8, LANES)),
            jnp.broadcast_to(ints_s[3, :, pl.ds(c * rays + (groups - 1) * LANES, LANES)], (8, LANES)),
        ) > 0

        def step_of(pair, item, item_first):
            run, run_t = pair
            item_t = spread(item)
            run_first = jnp.where(is_trans, 0.0, run) + run_t * item
            late_first = jnp.where(is_trans, 0.0, item) + item_t * run
            return jnp.where(item_first, late_first, run_first), run_t * item_t

        low = high = (identity, jnp.ones_like(identity))
        for s in range(n_slab):
            t = n_slab - 1 - s
            low = step_of(low, jnp.where(s < me, gather_s[s, c], identity), rev)
            high = step_of(high, jnp.where(t > me, gather_s[t, c], identity), jnp.logical_not(rev))
        low, low_t = low
        high, high_t = high
        own = send_s[c]
        front = jnp.where(rev, high, low)
        back = jnp.where(rev, low, high)
        front_t, own_t = jnp.where(rev, high_t, low_t), spread(own)
        logits = front + front_t * own + (front_t * own_t) * back
        shade = 1.0 / (1.0 + jnp.exp(-logits))
        target = jnp.zeros((8, LANES), jnp.float32)
        for g in range(groups):
            for k in range(3):
                target = jnp.where(
                    tile_rows == 4 * g + 1 + k,
                    target_s[k : k + 1, pl.ds(c * rays + g * LANES, LANES)],
                    target,
                )
        grad3 = jnp.where(is_trans, 0.0, (shade - target) * (1.0 / rays_dev) * shade * (1.0 - shade))
        seg = front_t * grad3
        dots = seg * back
        fronts, grads, seg_t = [], [[], [], []], []
        for g in range(groups):
            r = 4 * g
            fronts.append(front[r : r + 1, :])
            for k in range(3):
                grads[k].append(seg[r + 1 + k : r + 2 + k, :])
            seg_t.append(dots[r + 1 : r + 2, :] + dots[r + 2 : r + 3, :] + dots[r + 3 : r + 4, :])
        join = lambda parts: jnp.concatenate(parts, 1)
        front_out[:, rs] = join(fronts)
        return [join(grads[k]) for k in range(3)] + [join(seg_t)]

    def coefficients(c, cot):
        weights = saved_s[c, 0]
        density = (
            cot[0] * saved_s[c, 1] + cot[1] * saved_s[c, 2] + cot[2] * saved_s[c, 3] + cot[3] * saved_s[c, 4]
        )
        for m, value in enumerate([density] + [cot[k] * weights for k in range(3)]):
            hi = value.astype(jnp.bfloat16).astype(jnp.float32)
            for g in range(groups):
                for row, part in ((m, hi), (4 + m, value - hi), (8 + m, hi)):
                    stack_s[c, g, row * samples : (row + 1) * samples, :] = lanes_of(part, g)
        for j in range(samples):
            for g in range(groups):
                coef_s[:, pl.ds(c * cols + j * rays + g * LANES, LANES)] = jnp.concatenate(
                    [
                        stack_s[c, g, pl.ds(j, 8, stride=samples), :],
                        stack_s[c, g, pl.ds(8 * samples + j, 8, stride=samples), :],
                    ],
                    0,
                ).astype(jnp.bfloat16)

    def grad_out(cots):
        hid = h2_s.shape[0]
        block = 32
        column = lax.broadcasted_iota(jnp.int32, (block, LANES), 1)
        for f in range(0, hid, block):
            parts = [0.0] * 4
            for c in range(chunks):
                for g in range(groups):
                    at = pl.ds(g * LANES, LANES)
                    shown = held_s[c, 0, f : f + block, at]
                    for k in range(3):
                        parts[k] = parts[k] + shown * lanes_of(cots[c][k], g)
                    for m in range(4):
                        parts[3] = parts[3] + held_s[c, 1 + m, f : f + block, at] * lanes_of(cots[c][m], g)
            packed = jnp.zeros((block, LANES), jnp.float32)
            for k in range(4):
                packed = jnp.where(column == k, jnp.sum(parts[k], axis=1, keepdims=True), packed)
            held_s[0, 0, f : f + block, 0:LANES] = packed
        sums = held_s[0, 0, :, 0:LANES].T
        first_row = lax.broadcasted_iota(jnp.int32, (width, 1), 0) == 0
        total = jnp.where(first_row, sums[3:4, :], 0.0)
        for k in range(3):
            total = total + headt_s[0:width, 1 + k : 2 + k] * sums[k : k + 1, :]
        g3_s[...] = total

    def backward_two(c):
        base = c * cols
        b2 = mm(foldt_s[...], coef_s[:, pl.ds(base, cols)], NN).astype(jnp.bfloat16)
        b2 = jnp.where(h2_s[:, pl.ds(base, cols)] > 0, b2, 0)
        b2_s[:, pl.ds(base, cols)] = b2
        part = mm(h1_s[:, pl.ds(base, cols)], b2, NT)
        g2_s[...] = part if c == 0 else g2_s[...] + part

    def backward_one(c):
        base = c * cols
        b1 = mm(w2_s[...], b2_s[:, pl.ds(base, cols)], NN).astype(jnp.bfloat16)
        b1 = jnp.where(h1_s[:, pl.ds(base, cols)] > 0, b1, 0)
        part = mm(x_s[c].reshape(cols, x_s.shape[3]), b1, ((0,), (1,)))
        g1_s[...] = part if c == 0 else g1_s[...] + part

    grads = (
        (g1_s, pair1_s, near1_s, mid1_s, far1_s, other1_s, g1_out),
        (g2_s, pair2_s, near2_s, mid2_s, far2_s, None, g2_out),
        (g3_s, pair3_s, near3_s, mid3_s, far3_s, other3_s, g3_out),
    )
    partner = ypos * 2 + 1 - core

    def half_rows(i, k):
        rows = grads[i][1].shape[0]
        return pl.ds(pl.multiple_of(k * rows, 8), rows)

    def part_rows(i, part):
        rows = grads[i][1].shape[0] // 2
        return pl.ds(part * rows, rows)

    def pair_copy(i):
        whole, pair = grads[i][:2]
        return pltpu.make_async_remote_copy(
            src_ref=whole.at[half_rows(i, 1 - core), :],
            dst_ref=pair,
            send_sem=pair_send.at[i],
            recv_sem=pair_recv.at[i],
            device_id={"tile": partner},
            device_id_type=MESH,
        )

    def swap_copy(i, stage, part, turn):
        whole, pair, near, mid, far = grads[i][:5]
        rows = pair.shape[0] // 2
        if stage == 0 and i == 1:
            source, target = half2_s.at[part_rows(i, part), :], near
        elif stage == 0:
            half = 1 - core if turn else core
            at = pl.multiple_of(half * (2 * rows) + part * rows, 8)
            source, target = whole.at[pl.ds(at, rows), :], near
        else:
            source, target = mid.at[part_rows(i, part), :], far
        return pltpu.make_async_remote_copy(
            src_ref=source,
            dst_ref=target.at[turn, part_rows(i, part), :],
            send_sem=swap_send.at[i, stage, part, turn],
            recv_sem=swap_recv.at[i, stage, part, turn],
            device_id={"tile": across[(stage + part) % 2] * 2 + (1 - core if turn else core)},
            device_id_type=MESH,
        )

    def pass_copy(i):
        source, target = grads[i][3], grads[i][5]
        if i == 1:
            source = target = g2_out.at[half_rows(1, core), :]
        return pltpu.make_async_remote_copy(
            src_ref=source,
            dst_ref=target,
            send_sem=pass_send.at[i],
            recv_sem=pass_recv.at[i],
            device_id={"tile": partner},
            device_id_type=MESH,
        )

    def send_own(i):
        for turn in range(2):
            for part in range(2):
                swap_copy(i, 0, part, turn).start()
        pair_copy(i).start()

    def send_sums(i):
        whole, pair, near, mid = grads[i][:4]
        rows = pair.shape[0] // 2
        pair_copy(i).wait_recv()
        for part in range(2):
            for turn in range(2):
                swap_copy(i, 0, part, turn).wait_recv()
            at = part_rows(i, part)
            own = whole[pl.ds(pl.multiple_of(core * (2 * rows) + part * rows, 8), rows), :]
            mid[at, :] = (own + pair[at, :]) + (near[0, at, :] + near[1, at, :])
            for turn in range(2):
                swap_copy(i, 1, part, turn).start()
        pass_copy(i).start()

    def lean_first():
        pair_copy(1).wait_recv()
        half2_s[...] = g2_s[half_rows(1, core), :] + pair2_s[...]
        for part in range(2):
            swap_copy(1, 0, part, 0).start()

    def lean_second():
        for part in range(2):
            swap_copy(1, 0, part, 0).wait_recv()
            at = part_rows(1, part)
            mid2_s[at, :] = half2_s[at, :] + near2_s[0, at, :]
            swap_copy(1, 1, part, 0).start()

    def lean_third():
        for part in range(2):
            swap_copy(1, 1, part, 0).wait_recv()
        g2_out[half_rows(1, core), :] = mid2_s[...] + far2_s[0]
        pass_copy(1).start()

    def finish(i):
        mid, far, other, out = grads[i][3:]
        for turn in range(2):
            for part in range(2):
                swap_copy(i, 1, part, turn).wait_recv()
        out[half_rows(i, core), :] = mid[...] + far[0]
        pass_copy(i).wait_recv()
        out[half_rows(i, 1 - core), :] = other[...] + far[1]

    for c in range(chunks):
        forward_samples(c)
    values = [forward_rays(c) for c in range(chunks)]
    pl.semaphore_wait(barrier, n_slab - 1 + len(mates))
    for step in range(n_slab - 1):
        exchange(step, me).start()
    gather_s[me] = send_s[...]
    for c in range(chunks):
        slopes(c, values[c])
    for c in range(chunks):
        hold(c)
    for step in range(n_slab - 1):
        exchange(step, origin(step)).wait_recv()
    cots = [compose(c) for c in range(chunks)]
    for c in range(chunks):
        coefficients(c, cots[c])
    backward_two(0)
    grad_out(cots)
    send_own(2)
    backward_two(1)
    pair_copy(1).start()
    backward_one(0)
    lean_first()
    backward_one(1)
    send_own(0)
    send_sums(2)
    lean_second()
    send_sums(0)
    finish(2)
    lean_third()
    finish(0)
    pass_copy(1).wait_recv()
    for i in (2, 1, 0):
        pass_copy(i).wait_send()
        pair_copy(i).wait_send()
        for stage in range(2):
            for part in range(2):
                for turn in range(1 if i == 1 else 2):
                    swap_copy(i, stage, part, turn).wait_send()
    for step in range(n_slab - 1):
        exchange(step, me).wait_send()


def hand_on(*refs):
    half = len(refs) // 2
    for src, dst in zip(refs[:half], refs[half:]):
        dst[...] = src[...]


def solution(mesh):
    n_slab, n_tile = mesh.shape["slab"], mesh.shape["tile"]
    chunks = 2

    def body(
        encoded,
        spacing,
        counts,
        seg_first,
        seg_last,
        direction,
        field_in,
        field_mid,
        field_out,
        color_head,
        target,
    ):
        _, samples, rays_dev, enc = encoded.shape
        hid, out = field_out.shape[1:]
        rays = rays_dev // chunks
        total = samples * rays_dev
        f32, bf16 = jnp.float32, jnp.bfloat16
        row = lambda v: v.reshape(1, rays_dev)
        sizes = ((enc, hid), (hid, hid), (out, hid))
        any_space = pl.BlockSpec(memory_space=pl.ANY)
        vmem = pl.BlockSpec(memory_space=pltpu.VMEM)
        scratch = [
            pltpu.VMEM((chunks, samples, rays, enc), bf16),
            pltpu.VMEM((samples, rays_dev), f32),
            pltpu.VMEM((4, 1, rays_dev), jnp.int32),
            pltpu.VMEM((enc, hid), bf16),
            pltpu.VMEM((hid, hid), bf16),
            pltpu.VMEM((out, hid), bf16),
            pltpu.VMEM((3, out), f32),
            pltpu.VMEM((3, rays_dev), f32),
            pltpu.VMEM((hid, enc), bf16),
            pltpu.VMEM((hid, hid), bf16),
            pltpu.VMEM((8, LANES), f32),
            pltpu.VMEM((LANES, 8), f32),
            pltpu.VMEM((32, hid), bf16),
            pltpu.VMEM((LANES, hid), f32),
            pltpu.VMEM((hid, 16), bf16),
            pltpu.VMEM((hid, total), bf16),
            pltpu.VMEM((hid, total), bf16),
            pltpu.VMEM((hid, total), bf16),
            pltpu.VMEM((16, total), bf16),
            pltpu.VMEM((chunks, rays // LANES, 8 * samples, LANES), f32),
            pltpu.VMEM((chunks, rays // LANES, 16 * samples, LANES), f32),
            pltpu.VMEM((chunks, 5, samples, rays), f32),
            pltpu.VMEM((chunks, 5, hid, rays), f32),
            pltpu.VMEM((chunks, 8, LANES), f32),
            pltpu.VMEM((n_slab, chunks, 8, LANES), f32),
            pltpu.VMEM((enc, hid), f32),
            pltpu.VMEM((hid, hid), f32),
            pltpu.VMEM((out, hid), f32),
            *(pltpu.VMEM((r // 2, n), f32) for r, n in sizes),
            *(pltpu.VMEM((r // 2, n), f32) for r, n in sizes),
            *(pltpu.VMEM((2, r // 2, n), f32) for r, n in sizes),
            *(pltpu.VMEM((2, r // 2, n), f32) for r, n in sizes),
            *(pltpu.VMEM((r // 2, n), f32) for r, n in sizes[::2]),
            pltpu.VMEM((hid // 2, hid), f32),
            pltpu.SemaphoreType.DMA((chunks + 10,)),
            pltpu.SemaphoreType.DMA((n_slab,)),
            pltpu.SemaphoreType.DMA((n_slab,)),
            pltpu.SemaphoreType.DMA((3,)),
            pltpu.SemaphoreType.DMA((3,)),
            pltpu.SemaphoreType.DMA((3, 2, 2, 2)),
            pltpu.SemaphoreType.DMA((3, 2, 2, 2)),
            pltpu.SemaphoreType.DMA((3,)),
            pltpu.SemaphoreType.DMA((3,)),
        ]
        shapes = (
            jax.ShapeDtypeStruct((1, rays_dev), f32),
            jax.ShapeDtypeStruct((enc, hid), f32),
            jax.ShapeDtypeStruct((hid, hid), f32),
            jax.ShapeDtypeStruct((out, hid), f32),
        )
        results = pl.pallas_call(
            functools.partial(kernel, chunks, n_slab, n_tile),
            out_shape=tuple(pltpu.VMEM(q.shape, q.dtype) for q in shapes),
            in_specs=[any_space] * 11,
            out_specs=(vmem,) * 4,
            scratch_shapes=scratch,
            compiler_params=pltpu.CompilerParams(
                collective_id=0, has_side_effects=True, vmem_limit_bytes=56 * 2**20
            ),
        )(
            encoded,
            spacing,
            counts,
            row(seg_first),
            row(seg_last),
            row(direction),
            field_in,
            field_mid,
            field_out.transpose(0, 2, 1),
            color_head.T,
            target.T,
        )
        front, g1, g2, g3t = pl.pallas_call(
            hand_on,
            out_shape=shapes,
            in_specs=[vmem] * 4,
            out_specs=(vmem,) * 4,
        )(*(pltpu.with_memory_space_constraint(r, pltpu.VMEM) for r in results))
        return front, g1[None], g2[None], g3t.T[None]

    return jax.shard_map(
        body,
        mesh=mesh,
        in_specs=(
            P("slab", None, "tile", None),
            P("slab", None, "tile"),
            P("slab", "tile"),
            P("tile"),
            P("tile"),
            P("tile"),
            P("slab", None, None),
            P("slab", None, None),
            P("slab", None, None),
            P(),
            P("tile", None),
        ),
        out_specs=(
            P("slab", "tile"),
            P("slab", None, None),
            P("slab", None, None),
            P("slab", None, None),
        ),
        check_vma=False,
    )
```
